32 devices in a mesh: gy: 16 (over z, x, core), gz: 2 (over y).
Axes of the slice: x: 2, y: 2, z: 4, core: 2. Of those that a mesh axis runs over, the one named last changes fastest.
Arguments:
- moments: float32 [10, 4, 16, 4096], P(None, 'gz', 'gy'), may hold values from -0.5 to 1.2, as said below
- wavenumbers: int32 [3, 2048], replicated, may hold values from 0 to 31
- mode_gain: float32 [2048], replicated, may hold values from 0.2 to 2
Outputs:
- final_moments: float32 [10, 4, 16, 4096], P(None, 'gz', 'gy')
- mode_coeffs: float32 [2, 3, 2048], replicated
The draws below stay inside these ranges and needn't reach their ends.
Inputs may be any that keep to these rules, and one draw needn't show every extreme that they name: `moments`: density lies in 0.85 to 1.15 in every cell and each component of j / rho is below 0.2 in magnitude.
All inputs are finite; a program needn't handle non-finite values.
Results may differ from the reference program's by a relative error of at most 0.0003.
Values sent between devices are 32-bit elements; how exact they have to be, the bound alone decides.
A program may use at most 64 MiB of HBM per device.

```python
import math
import jax
import jax.numpy as jnp
from jax import lax

NX = 4096
CZ = 2
K = 2048
KMAX = 32
STEPS = 3
NY = 16
NZ = 4
N_GY = 16
N_GZ = 2


PAIR_LIST = ((0, 0), (1, 1), (2, 2), (0, 1), (0, 2), (1, 2))


MODE_AMPLITUDE = 0.02


def common_waves(key):
    waves = jax.random.randint(jax.random.fold_in(key, 5), (3, K), 0, KMAX, dtype=jnp.int32)
    waves = waves.at[0, 0].set(0)
    waves = waves.at[0, 1].set(KMAX - 1)
    return waves


def draw_wavenumbers(key, part):
    return common_waves(key)


def draw_moments(key, part):
    waves = common_waves(key)
    subkeys = jax.random.split(jax.random.fold_in(key, 11), 3)
    grid_shape = (NZ, NY, NX)
    density = jax.random.uniform(subkeys[0], grid_shape, jnp.float32, 0.85, 1.15)
    noise = jnp.clip(0.015 * jax.random.normal(subkeys[1], (3,) + grid_shape, jnp.float32), -0.04, 0.04)
    x_pos = jnp.arange(NX, dtype=jnp.int32)[None, None, :]
    y_pos = jnp.arange(NY, dtype=jnp.int32)[None, :, None]
    z_pos = jnp.arange(NZ, dtype=jnp.int32)[:, None, None]
    envelope = 1.0 + 0.9 * jnp.cos(2.0 * math.pi * y_pos.astype(jnp.float32) / NY)
    coherent = jnp.zeros(grid_shape, jnp.float32)
    for index_m in range(4):
        fraction = (x_pos * waves[0, index_m] % NX).astype(jnp.float32) / NX
        fraction = fraction + (y_pos * waves[1, index_m] % NY).astype(jnp.float32) / NY
        fraction = fraction + (z_pos * waves[2, index_m] % NZ).astype(jnp.float32) / NZ
        coherent = coherent + jnp.cos(2.0 * math.pi * fraction)
    coherent = MODE_AMPLITUDE * envelope * coherent
    velocity_field = noise + coherent[None]
    nonequil = jnp.clip(0.01 * jax.random.normal(subkeys[2], (6,) + grid_shape, jnp.float32), -0.04, 0.04)
    components = [density] + [density * velocity_field[comp_a] for comp_a in range(3)]
    for index_p, (comp_a, comp_b) in enumerate(PAIR_LIST):
        second = density * velocity_field[comp_a] * velocity_field[comp_b] + nonequil[index_p]
        if comp_a == comp_b:
            second = second + density / 3.0
        components.append(second)
    return jnp.stack(components).astype(jnp.float32)


def setup_inputs(seed: int = 0) -> dict:
    seeds = jax.random.split(jax.random.key(seed), 4)
    moments = draw_moments(jax.random.fold_in(seeds[3], 71), 0)
    wavenumbers = draw_wavenumbers(jax.random.fold_in(seeds[3], 71), 0)
    mode_gain = jnp.clip(jnp.exp(jax.random.uniform(seeds[2], (K,), jnp.float32, math.log(0.2), math.log(2.0))), 0.2, 2.0)
    return {"moments": moments, "wavenumbers": wavenumbers, "mode_gain": mode_gain}


VELOCITIES = ((0, 0, 0), (1, 0, 0), (-1, 0, 0), (0, 1, 0), (0, -1, 0), (0, 0, 1), (0, 0, -1), (1, 1, 0), (-1, -1, 0), (1, -1, 0), (-1, 1, 0), (1, 0, 1), (-1, 0, -1), (1, 0, -1), (-1, 0, 1), (0, 1, 1), (0, -1, -1), (0, 1, -1), (0, -1, 1))
PAIR_LIST = ((0, 0), (1, 1), (2, 2), (0, 1), (0, 2), (1, 2))
RELAX_RATE = 1.6
FORCE_GAIN = 0.5
HIGHEST = lax.Precision.HIGHEST

def lattice_weight(velocity):
    total = abs(velocity[0]) + abs(velocity[1]) + abs(velocity[2])
    if total == 0:
        return 1.0 / 3.0
    if total == 1:
        return 1.0 / 18.0
    return 1.0 / 36.0

def populate(moment_list, velocity):
    density = moment_list[0]
    linear = density
    for comp_a in range(3):
        if velocity[comp_a] != 0:
            linear = linear + 3.0 * velocity[comp_a] * moment_list[1 + comp_a]
    quadratic = jnp.zeros_like(density)
    for index_p, (comp_a, comp_b) in enumerate(PAIR_LIST):
        if comp_a == comp_b:
            factor = velocity[comp_a] * velocity[comp_a] - 1.0 / 3.0
            quadratic = quadratic + factor * (moment_list[4 + index_p] - density / 3.0)
        else:
            factor = 2.0 * velocity[comp_a] * velocity[comp_b]
            if factor != 0:
                quadratic = quadratic + factor * moment_list[4 + index_p]
    return lattice_weight(velocity) * (linear + 4.5 * quadratic)

def add_population(totals, population, velocity):
    totals[0] = totals[0] + population
    for comp_a in range(3):
        if velocity[comp_a] != 0:
            totals[1 + comp_a] = totals[1 + comp_a] + velocity[comp_a] * population
    for index_p, (comp_a, comp_b) in enumerate(PAIR_LIST):
        product = velocity[comp_a] * velocity[comp_b]
        if product != 0:
            totals[4 + index_p] = totals[4 + index_p] + product * population
    return totals

def collide(totals, force_field):
    density = totals[0]
    shifted = [(totals[1 + comp_a] + 0.5 * force_field[comp_a]) / density for comp_a in range(3)]
    result_list = [density] + [totals[1 + comp_a] + force_field[comp_a] for comp_a in range(3)]
    for index_p, (comp_a, comp_b) in enumerate(PAIR_LIST):
        equilibrium = density * shifted[comp_a] * shifted[comp_b]
        if comp_a == comp_b:
            equilibrium = equilibrium + density / 3.0
        result_list.append(equilibrium + (1.0 - RELAX_RATE) * (totals[4 + index_p] - equilibrium))
    return jnp.stack(result_list)

def phase_x(positions, length):
    wave_list = jnp.arange(KMAX, dtype=jnp.int32)
    fraction = (positions[:, None] * wave_list[None, :] % length).astype(jnp.float32) / length
    phase_angle = 2.0 * math.pi * fraction
    return jnp.concatenate([jnp.cos(phase_angle), jnp.sin(phase_angle)], axis=1)

def select_table(wavenumbers):
    wave_list = jnp.arange(KMAX, dtype=jnp.int32)
    return (wave_list[:, None] == wavenumbers[0][None, :]).astype(jnp.float32)

def phase_yz(wavenumbers, y_positions, y_length, z_positions, z_length):
    fraction = (y_positions[None, :, None] * wavenumbers[1][None, None, :] % y_length).astype(jnp.float32) / y_length
    fraction = fraction + (z_positions[:, None, None] * wavenumbers[2][None, None, :] % z_length).astype(jnp.float32) / z_length
    phase_angle = 2.0 * math.pi * fraction
    return (jnp.cos(phase_angle), jnp.sin(phase_angle))

def project(velocity_field, x_basis, selector, cos_yz, sin_yz):
    modes = cos_yz.shape[-1]
    depth, rows, cells_x = velocity_field.shape[1:]
    waves = x_basis.shape[1] // 2
    projected = jnp.dot(velocity_field.reshape(-1, cells_x), x_basis, precision=HIGHEST, preferred_element_type=jnp.float32)
    cos_x = jnp.dot(projected[:, :waves], selector, precision=HIGHEST, preferred_element_type=jnp.float32).reshape(3, depth, rows, modes)
    sin_x = jnp.dot(projected[:, waves:], selector, precision=HIGHEST, preferred_element_type=jnp.float32).reshape(3, depth, rows, modes)
    cos_sum = lax.optimization_barrier(jnp.sum(cos_x * cos_yz - sin_x * sin_yz, axis=(1, 2)))
    sin_sum = lax.optimization_barrier(jnp.sum(sin_x * cos_yz + cos_x * sin_yz, axis=(1, 2)))
    return jnp.stack([cos_sum, sin_sum])

def apply_force(scaled, x_basis, selector, cos_yz, sin_yz):
    depth, rows, modes = cos_yz.shape
    cos_part = scaled[0][:, None, None, :]
    sin_part = scaled[1][:, None, None, :]
    part_a = (cos_part * cos_yz + sin_part * sin_yz).reshape(-1, modes)
    part_b = (sin_part * cos_yz - cos_part * sin_yz).reshape(-1, modes)
    wave_a = jnp.dot(part_a, selector.T, precision=HIGHEST, preferred_element_type=jnp.float32)
    wave_b = jnp.dot(part_b, selector.T, precision=HIGHEST, preferred_element_type=jnp.float32)
    stacked = jnp.concatenate([wave_a, wave_b], axis=-1)
    return jnp.dot(stacked, x_basis.T, precision=HIGHEST, preferred_element_type=jnp.float32).reshape(3, depth, rows, x_basis.shape[0])

def reference(moments, wavenumbers, mode_gain):
    cells_z, cells_y, cells_x = moments.shape[1:]
    x_basis = phase_x(jnp.arange(cells_x, dtype=jnp.int32), cells_x)
    selector = select_table(wavenumbers)
    y_positions = jnp.arange(cells_y, dtype=jnp.int32)
    normalizer = 1.0 / math.sqrt(NX * NY * NZ)
    force_scale = FORCE_GAIN / math.sqrt(2 * K * N_GY * N_GZ)
    blocks = jnp.arange(cells_z // CZ, dtype=jnp.int32)
    moment_state = moments
    coeffs = jnp.zeros((2, 3, K), jnp.float32)
    for step_index in range(STEPS):
        velocity_field = moment_state[1:4] / moment_state[0]

        def block_tables(block_index):
            z_start = (block_index * CZ).astype(jnp.int32)
            z_positions = z_start + jnp.arange(CZ, dtype=jnp.int32)
            return (z_start, phase_yz(wavenumbers, y_positions, cells_y, z_positions, cells_z))

        def block_sum(block_index):
            z_start, tables = block_tables(block_index)
            piece = lax.dynamic_slice_in_dim(velocity_field, z_start, CZ, 1)
            return project(piece, x_basis, selector, tables[0], tables[1])
        coeffs = lax.optimization_barrier(jnp.sum(lax.map(block_sum, blocks), axis=0)) * normalizer
        scaled = coeffs * mode_gain[None, None, :] * force_scale

        def block_force(block_index):
            z_start, tables = block_tables(block_index)
            return apply_force(scaled, x_basis, selector, tables[0], tables[1])
        force_blocks = lax.map(block_force, blocks)
        force_field = jnp.transpose(force_blocks, (1, 0, 2, 3, 4)).reshape(3, cells_z, cells_y, cells_x)
        totals = [jnp.zeros((cells_z, cells_y, cells_x), jnp.float32) for index_p in range(10)]
        for velocity in VELOCITIES:
            population = populate(moment_state, velocity)
            read = jnp.roll(population, (velocity[2], velocity[1], velocity[0]), axis=(0, 1, 2))
            totals = add_population(totals, read, velocity)
        moment_state = collide(totals, force_field)
    return (moment_state, coeffs)
```

```python
import functools
import math

import jax
import jax.numpy as jnp
import numpy as np
from jax import lax
from jax.experimental import pallas as pl
from jax.experimental.pallas import tpu as pltpu
from jax.sharding import PartitionSpec as P

KMAX = 32
STEPS = 3
RELAX_RATE = 1.6
FORCE_GAIN = 0.5
LANES = 128
MESH = pl.DeviceIdType.MESH
F32 = jnp.float32
BF16 = jnp.bfloat16


def split_np(table):
    high = table.astype(np.float32).astype(jnp.bfloat16)
    low = (table.astype(np.float32) - high.astype(np.float32)).astype(jnp.bfloat16)
    return np.stack([high, low])


def split(value):
    high = value.astype(BF16)
    return high, (value - high.astype(F32)).astype(BF16)


def dot(lhs, rhs, lhs_dim, rhs_dim):
    return lax.dot_general(
        lhs, rhs, (((lhs_dim,), (rhs_dim,)), ((), ())), preferred_element_type=F32
    )


def dot3(lhs, rhs, lhs_dim, rhs_dim):
    return (
        dot(lhs[0], rhs[0], lhs_dim, rhs_dim)
        + dot(lhs[0], rhs[1], lhs_dim, rhs_dim)
        + dot(lhs[1], rhs[0], lhs_dim, rhs_dim)
    )


def modulo(value, count):
    if count & (count - 1) == 0:
        return value & (count - 1)
    return lax.rem(value, count)


def divide(value, count):
    if count & (count - 1) == 0:
        return lax.shift_right_logical(value, count.bit_length() - 1)
    return lax.div(value, count)


def wave_tables(cells_x):
    rows = cells_x // LANES
    k = np.arange(KMAX)
    alpha = 2 * np.pi * ((np.arange(rows)[:, None] * LANES * k) % cells_x) / cells_x
    phi = 2 * np.pi * ((np.arange(LANES)[:, None] * k) % cells_x) / cells_x
    ca, sa, cp, sp = np.cos(alpha), np.sin(alpha), np.cos(phi), np.sin(phi)
    forward = np.concatenate([ca, sa, -sa, ca], 1)
    forward_fine = np.concatenate([cp, cp, sp, sp], 1)
    inverse = np.concatenate([ca, ca, sa, sa], 1)
    inverse_fine = np.concatenate([cp, sp, cp, sp], 1)
    fine = np.stack([forward_fine, inverse_fine]).astype(np.float32)
    coarse = np.concatenate([split_np(forward), split_np(inverse)])
    return (jnp.asarray(coarse), jnp.asarray(fine))


def plane_tables(count_gy, count_gz, depth):
    length_y, length_z = count_gy, count_gz * depth
    waves_y, waves_z = min(KMAX, length_y), min(KMAX, length_z)
    device = np.arange(count_gy * count_gz)
    y = np.tile(device // count_gz, depth)
    z = np.concatenate([(device % count_gz) * depth + s for s in range(depth)])
    q = np.arange(waves_y * waves_z)
    phase = (y[:, None] * (q // waves_z) % length_y) / length_y
    phase = phase + (z[:, None] * (q % waves_z) % length_z) / length_z
    cos, sin = np.cos(2 * np.pi * phase), np.sin(2 * np.pi * phase)
    by_source = np.concatenate([cos, sin], 1)
    by_wave = np.concatenate([cos.T, sin.T], 1)
    return (jnp.asarray(split_np(by_source)), jnp.asarray(split_np(by_wave)))


def roll_x(value, shift, lane):
    rows = value.shape[0]
    if shift == 1:
        moved = pltpu.roll(value, 1, 1)
        return jnp.where(lane == 0, pltpu.roll(moved, 1, 0), moved)
    moved = pltpu.roll(value, LANES - 1, 1)
    return jnp.where(lane == LANES - 1, pltpu.roll(moved, rows - 1, 0), moved)


def populations(m, lane):
    rho, jx, jy, jz, pxx, pyy, pzz, pxy, pxz, pyz = m
    trace = 1.5 * (pxx + pyy + pzz)
    out = {(0, 0, 0): (2.5 * rho - trace) * (1.0 / 3.0)}
    base = rho - trace
    j = (jx, jy, jz)
    diag = (4.5 * pxx, 4.5 * pyy, 4.5 * pzz)
    for a in range(3):
        even = (base + diag[a]) * (1.0 / 18.0)
        odd = j[a] * (1.0 / 6.0)
        e = [0, 0, 0]
        e[a] = 1
        out[tuple(e)] = even + odd
        e[a] = -1
        out[tuple(e)] = even - odd
    base = -0.5 * rho - trace
    for a, b, cross in ((0, 1, pxy), (0, 2, pxz), (1, 2, pyz)):
        even = (base + (diag[a] + diag[b])) * (1.0 / 36.0)
        quarter = 0.25 * cross
        plus, minus = even + quarter, even - quarter
        total, diff = (j[a] + j[b]) * (1.0 / 12.0), (j[a] - j[b]) * (1.0 / 12.0)
        for sa, sb, value in (
            (1, 1, plus + total),
            (-1, -1, plus - total),
            (1, -1, minus + diff),
            (-1, 1, minus - diff),
        ):
            e = [0, 0, 0]
            e[a], e[b] = sa, sb
            out[tuple(e)] = value
    return {e: (roll_x(v, e[0], lane) if e[0] else v) for e, v in out.items()}


def gather_totals(g):
    s, d = [], []
    for a in range(3):
        e = [0, 0, 0]
        e[a] = 1
        up = g[tuple(e)]
        e[a] = -1
        down = g[tuple(e)]
        s.append(up + down)
        d.append(up - down)
    s1, d1, s2, d2 = {}, {}, {}, {}
    for a, b in ((0, 1), (0, 2), (1, 2)):
        get = {}
        for sa in (1, -1):
            for sb in (1, -1):
                e = [0, 0, 0]
                e[a], e[b] = sa, sb
                get[(sa, sb)] = g[tuple(e)]
        s1[a, b] = get[1, 1] + get[-1, -1]
        d1[a, b] = get[1, 1] - get[-1, -1]
        s2[a, b] = get[1, -1] + get[-1, 1]
        d2[a, b] = get[1, -1] - get[-1, 1]
    both = {key: s1[key] + s2[key] for key in s1}
    rho = g[0, 0, 0] + (s[0] + s[1] + s[2]) + (both[0, 1] + both[0, 2] + both[1, 2])
    jx = d[0] + (d1[0, 1] + d2[0, 1]) + (d1[0, 2] + d2[0, 2])
    jy = d[1] + (d1[0, 1] - d2[0, 1]) + (d1[1, 2] + d2[1, 2])
    jz = d[2] + (d1[0, 2] - d2[0, 2]) + (d1[1, 2] - d2[1, 2])
    pxx = s[0] + both[0, 1] + both[0, 2]
    pyy = s[1] + both[0, 1] + both[1, 2]
    pzz = s[2] + both[0, 2] + both[1, 2]
    return [rho, jx, jy, jz, pxx, pyy, pzz] + [s1[k] - s2[k] for k in ((0, 1), (0, 2), (1, 2))]


PAIR_LIST = ((0, 0), (1, 1), (2, 2), (0, 1), (0, 2), (1, 2))


def collide(totals, force):
    density = totals[0]
    inverse = 1.0 / density
    shifted = [(totals[1 + a] + 0.5 * force[a]) * inverse for a in range(3)]
    result = [density] + [totals[1 + a] + force[a] for a in range(3)]
    third = density * (1.0 / 3.0)
    for index, (a, b) in enumerate(PAIR_LIST):
        equilibrium = density * shifted[a] * shifted[b]
        if a == b:
            equilibrium = equilibrium + third
        result.append(
            RELAX_RATE * equilibrium + (1.0 - RELAX_RATE) * totals[4 + index]
        )
    return result


def kernel(
    count_gy, count_gz, gain_scale, normalizer,
    moments_in, wavenumbers_in, gain_in, coarse_in, fine_in, source_in, wave_in,
    final, coeffs,
    moments, wavenumbers, gain, coarse_tables, fine, source_tables, wave_tables_ref,
    load, state, gathered, filters, send_y, send_z, send_d, recv_y, recv_z, recv_d,
    gather_send, gather_recv, halo_send, halo_recv,
):
    depth, rows = moments.shape[1:3]
    devices = count_gy * count_gz
    my_y, my_z = lax.axis_index("gy"), lax.axis_index("gz")
    me = my_y * count_gz + my_z
    lane = lax.broadcasted_iota(jnp.int32, (rows, LANES), 1)
    lane1 = lax.broadcasted_iota(jnp.int32, (1, LANES), 1)

    def peer(i):
        if devices & (devices - 1) == 0:
            target = me ^ i
        else:
            target = modulo(me + i, devices)
        return (divide(target, count_gz), modulo(target, count_gz))

    barrier = pltpu.get_barrier_semaphore()

    def greet(i, carry):
        pl.semaphore_signal(barrier, inc=1, device_id=peer(devices - i), device_id_type=MESH)
        return carry

    lax.fori_loop(1, devices, greet, 0)

    loads = [
        pltpu.make_async_copy(src, dst, load.at[i])
        for i, (src, dst) in enumerate((
            (moments_in, moments), (coarse_in, coarse_tables), (fine_in, fine),
            (wavenumbers_in, wavenumbers), (gain_in, gain), (source_in, source_tables),
            (wave_in, wave_tables_ref),
        ))
    ]
    for copy in loads:
        copy.start()

    def y_at(step):
        return modulo(my_y + step + count_gy, count_gy)

    def z_at(step):
        return modulo(my_z + step + count_gz, count_gz)

    def remote(src, dst, step, index, target):
        return pltpu.make_async_remote_copy(
            src_ref=src, dst_ref=dst,
            send_sem=halo_send.at[step, index], recv_sem=halo_recv.at[step, index],
            device_id=target, device_id_type=MESH,
        )

    def halo_copies(step):
        out = []
        for i, sy in enumerate((1, -1)):
            out.append(remote(send_y.at[step, i], recv_y.at[step, i], step, i, (y_at(sy), my_z)))
        for i, sz in enumerate((1, -1)):
            out.append(
                remote(send_z.at[step, i], recv_z.at[step, i], step, 2 + i, (my_y, z_at(sz)))
            )
        for i, sy in enumerate((1, -1)):
            for k, sz in enumerate((1, -1)):
                c = 2 * i + k
                out.append(
                    remote(
                        send_d.at[step, c], recv_d.at[step, c], step, 4 + c, (y_at(sy), z_at(sz))
                    )
                )
        return out

    waves_y, waves_z = min(KMAX, count_gy), min(KMAX, count_gz * depth)
    modes = wavenumbers.shape[1]

    def wave_onehot():
        q = modulo(wavenumbers[1:2, :], count_gy) * waves_z
        q = q + modulo(wavenumbers[2:3, :], count_gz * depth)
        index = lax.broadcasted_iota(jnp.int32, (waves_y * waves_z, modes), 0)
        return jnp.where(index == q, 1.0, 0.0)

    def x_onehot():
        index = lax.broadcasted_iota(jnp.int32, (KMAX, modes), 0)
        return jnp.where(index == wavenumbers[0:1, :], 1.0, 0.0)

    def build_filters():
        count_q = waves_y * waves_z
        onehot_q = wave_onehot()
        weighted = split(onehot_q * gain[...])
        onehot_x = x_onehot().astype(BF16)
        onehot_x = jnp.concatenate([onehot_x] * 4, 0)
        energy = dot(weighted[0], onehot_x, 1, 1) + dot(weighted[1], onehot_x, 1, 1)
        energy = energy * gain_scale
        index = lax.broadcasted_iota(jnp.int32, (count_q, LANES), 0)
        wave_y, wave_z = divide(index, waves_z), modulo(index, waves_z)
        length_z = count_gz * depth
        phase_y = modulo(wave_y * my_y, count_gy).astype(F32) * (1.0 / count_gy)
        for t in range(depth):
            phase = modulo(wave_z * (my_z * depth + t), length_z).astype(F32)
            angle = (2.0 * math.pi) * (phase_y + phase * (1.0 / length_z))
            ec, es = energy * jnp.cos(angle), energy * jnp.sin(angle)
            for part, stack in enumerate(((ec, es), (es, -ec))):
                pieces = split(jnp.concatenate(stack, 0))
                table = dot3((source_tables[0], source_tables[1]), pieces, 1, 0)
                filters[2 * t + part] = jnp.where(
                    lane1 < LANES // 2, table[:devices], table[devices:]
                )

    def store_coeffs(spectra):
        half = LANES // 2
        sign = jnp.where((lane1 & KMAX) == 0, -1.0, 1.0)
        blocks = []
        for a in range(3):
            top = jnp.concatenate([spectra[a], pltpu.roll(spectra[a], half, 1)], 0)
            swapped = jnp.where((lane1 & KMAX) == 0, pltpu.roll(top, LANES - KMAX, 1), pltpu.roll(top, KMAX, 1))
            blocks.append(jnp.concatenate([top, sign * swapped], 0)[:, :half])
        stacked = jnp.concatenate(blocks, 1)
        transform = dot3((wave_tables_ref[0], wave_tables_ref[1]), split(stacked), 1, 0) * normalizer
        pieces = split(transform)
        onehot_q = wave_onehot().astype(BF16)
        chosen = dot(pieces[0], onehot_q, 0, 0) + dot(pieces[1], onehot_q, 0, 0)
        onehot_x = x_onehot()
        for a in range(3):
            for part in range(2):
                start = (2 * a + part) * KMAX
                picked = jnp.sum(chosen[start : start + KMAX] * onehot_x, axis=0, keepdims=True)
                coeffs[a, part : part + 1, :] = picked

    for copy in loads[:3]:
        copy.wait()
    source = moments
    for step in range(STEPS):
        layers = [[source[i, z] for i in range(10)] for z in range(depth)]
        speed = []
        for z in range(depth):
            inverse = 1.0 / layers[z][0]
            speed.append([layers[z][1 + a] * inverse for a in range(3)])
        stacked = jnp.concatenate([speed[z][a] for z in range(depth) for a in range(3)], 1)
        coarse = dot3(split(stacked), (coarse_tables[0], coarse_tables[1]), 0, 0)
        table = fine[0]
        folded = []
        for r in range(3 * depth):
            part = jnp.sum(coarse[r * LANES : (r + 1) * LANES] * table, axis=0, keepdims=True)
            folded.append(part + pltpu.roll(part, LANES // 2, 1))
        packed = [jnp.where(lane1 < LANES // 2, folded[a], folded[3 + a]) for a in range(3)]
        for a in range(3):
            gathered[step, me, :, a * LANES : (a + 1) * LANES] = packed[a]

        pops = [populations(layers[z], lane) for z in range(depth)]
        for i, sy in enumerate((1, -1)):
            for z in range(2):
                for n, sx in enumerate((0, 1, -1)):
                    send_y[step, i, 3 * z + n] = pops[z][sx, sy, 0]
            send_y[step, i, 6] = pops[0][0, sy, 1]
            send_y[step, i, 7] = pops[1][0, sy, -1]
            send_d[step, 2 * i] = pops[1][0, sy, 1]
            send_d[step, 2 * i + 1] = pops[0][0, sy, -1]
        for n, sx in enumerate((0, 1, -1)):
            send_z[step, 0, n] = pops[1][sx, 0, 1]
            send_z[step, 1, n] = pops[0][sx, 0, -1]

        if step == 0:
            pl.semaphore_wait(barrier, devices - 1)

        def send(i, carry, step=step):
            pltpu.make_async_remote_copy(
                src_ref=gathered.at[step, me], dst_ref=gathered.at[step, me],
                send_sem=gather_send.at[step], recv_sem=gather_recv.at[step],
                device_id=peer(devices - i), device_id_type=MESH,
            ).start()
            return carry

        copies = halo_copies(step)
        for copy in copies[4:]:
            copy.start()
        lax.fori_loop(1, devices, send, 0)

        for copy in copies[:4]:
            copy.start()

        if step == 0:
            for copy in loads[3:]:
                copy.wait()
            build_filters()

        others = gathered.at[step, pl.ds(0, devices - 1)]
        pltpu.make_async_copy(others, others, gather_recv.at[step]).wait()

        spectra = [gathered[step, :, 0, a * LANES : (a + 1) * LANES] for a in range(3)]
        inverse_fine = fine[1]
        swap_sign = jnp.where((lane1 & KMAX) == 0, 1.0, -1.0)
        outer_sign = jnp.where(lane1 < 3 * KMAX, 1.0, -1.0)
        expanded = []
        for z in range(depth):
            for a in range(3):
                first = jnp.sum(spectra[a] * filters[2 * z], axis=0, keepdims=True)
                second = jnp.sum(spectra[a] * filters[2 * z + 1], axis=0, keepdims=True)
                first = first + pltpu.roll(first, LANES // 2, 1)
                second = second + pltpu.roll(second, LANES // 2, 1)
                both = first + swap_sign * pltpu.roll(second, KMAX, 1)
                row = jnp.where(
                    lane1 < LANES // 2, both, outer_sign * pltpu.roll(both, KMAX, 1)
                )
                expanded.append(inverse_fine * row)
        force = dot3(
            (coarse_tables[2], coarse_tables[3]), split(jnp.concatenate(expanded, 0)), 1, 1
        )
        if step == STEPS - 1:
            store_coeffs(spectra)
        target = final if step == STEPS - 1 else state.at[step]
        for copy in copies:
            copy.wait_recv()
        for z in range(depth):
            g = {}
            for sx in (0, 1, -1):
                g[sx, 0, 0] = pops[z][sx, 0, 0]
            for n, sx in enumerate((0, 1, -1)):
                g[sx, 0, 1] = pops[0][sx, 0, 1] if z == 1 else recv_z[step, 0, n]
                g[sx, 0, -1] = pops[1][sx, 0, -1] if z == 0 else recv_z[step, 1, n]
            for i, sy in enumerate((1, -1)):
                for n, sx in enumerate((0, 1, -1)):
                    g[sx, sy, 0] = recv_y[step, i, 3 * z + n]
                g[0, sy, 1] = recv_y[step, i, 6] if z == 1 else recv_d[step, 2 * i]
                g[0, sy, -1] = recv_y[step, i, 7] if z == 0 else recv_d[step, 2 * i + 1]
            totals = gather_totals(g)
            pieces = [
                force[:, (3 * z + a) * LANES : (3 * z + a + 1) * LANES] for a in range(3)
            ]
            result = collide(totals, pieces)
            for i in range(10):
                target[i, z] = result[i]
        source = target

    for step in range(STEPS):
        others = gathered.at[step, pl.ds(0, devices - 1)]
        pltpu.make_async_copy(others, others, gather_send.at[step]).wait()
        for copy in halo_copies(step):
            copy.wait_send()


def hand_over(final_in, coeffs_in, final_out, coeffs_out, sems):
    copies = [
        pltpu.make_async_copy(final_in, final_out, sems.at[0]),
        pltpu.make_async_copy(coeffs_in, coeffs_out, sems.at[1]),
    ]
    for copy in copies:
        copy.start()
    for copy in copies:
        copy.wait()


def per_device(count_gy, count_gz, moments, wavenumbers, mode_gain):
    depth, height, cells_x = moments.shape[1:]
    assert height == 1 and depth == 2 and cells_x % 1024 == 0
    rows = cells_x // LANES
    modes = mode_gain.shape[0]
    devices = count_gy * count_gz
    normalizer = 1.0 / math.sqrt(cells_x * height * depth * devices)
    force_scale = FORCE_GAIN / math.sqrt(2 * modes * devices)
    tables = wave_tables(cells_x) + plane_tables(count_gy, count_gz, depth)
    operands = (moments.reshape(10, depth, rows, LANES), wavenumbers, mode_gain.reshape(1, modes)) + tables
    vmem = pl.BlockSpec(memory_space=pltpu.VMEM)
    final, coeffs = pl.pallas_call(
        functools.partial(kernel, count_gy, count_gz, force_scale * normalizer, normalizer),
        out_shape=(
            pltpu.VMEM((10, depth, rows, LANES), F32),
            pltpu.VMEM((3, 2, modes), F32),
        ),
        in_specs=[pl.BlockSpec(memory_space=pl.ANY)] * len(operands),
        out_specs=(vmem, vmem),
        scratch_shapes=[pltpu.VMEM(x.shape, x.dtype) for x in operands] + [
            pltpu.SemaphoreType.DMA((len(operands),)),
            pltpu.VMEM((STEPS - 1, 10, depth, rows, LANES), F32),
            pltpu.VMEM((STEPS, devices, 1, 3 * LANES), F32),
            pltpu.VMEM((2 * depth, devices, LANES), F32),
            pltpu.VMEM((STEPS, 2, 8, rows, LANES), F32),
            pltpu.VMEM((STEPS, 2, 3, rows, LANES), F32),
            pltpu.VMEM((STEPS, 4, rows, LANES), F32),
            pltpu.VMEM((STEPS, 2, 8, rows, LANES), F32),
            pltpu.VMEM((STEPS, 2, 3, rows, LANES), F32),
            pltpu.VMEM((STEPS, 4, rows, LANES), F32),
            pltpu.SemaphoreType.DMA((STEPS,)),
            pltpu.SemaphoreType.DMA((STEPS,)),
            pltpu.SemaphoreType.DMA((STEPS, 8)),
            pltpu.SemaphoreType.DMA((STEPS, 8)),
        ],
        compiler_params=pltpu.CompilerParams(
            collective_id=0, has_side_effects=True, vmem_limit_bytes=60 * 1024 * 1024
        ),
    )(*operands)
    final, coeffs = pl.pallas_call(
        hand_over,
        out_shape=(
            jax.ShapeDtypeStruct(final.shape, F32),
            jax.ShapeDtypeStruct(coeffs.shape, F32),
        ),
        in_specs=[vmem] * 2,
        out_specs=(pl.BlockSpec(memory_space=pl.ANY), pl.BlockSpec(memory_space=pl.ANY)),
        scratch_shapes=[pltpu.SemaphoreType.DMA((2,))],
        compiler_params=pltpu.CompilerParams(vmem_limit_bytes=4 * 1024 * 1024),
    )(final, coeffs)
    return final.reshape(moments.shape), jnp.transpose(coeffs, (1, 0, 2))


def solution(mesh):
    in_specs = (P(None, "gz", "gy", None), P(), P())
    out_specs = (P(None, "gz", "gy", None), P())
    body = functools.partial(per_device, mesh.shape["gy"], mesh.shape["gz"])
    return jax.shard_map(
        body, mesh=mesh, in_specs=in_specs, out_specs=out_specs, check_vma=False
    )
```

```python
import functools
import math

import jax
import jax.numpy as jnp
import numpy as np
from jax import lax
from jax.experimental import pallas as pl
from jax.experimental.pallas import tpu as pltpu
from jax.sharding import PartitionSpec as P

KMAX = 32
STEPS = 3
RELAX_RATE = 1.6
FORCE_GAIN = 0.5
LANES = 128
MESH = pl.DeviceIdType.MESH
F32 = jnp.float32
BF16 = jnp.bfloat16


def split_np(table):
    high = table.astype(np.float32).astype(jnp.bfloat16)
    low = (table.astype(np.float32) - high.astype(np.float32)).astype(jnp.bfloat16)
    return np.stack([high, low])


def paired(table):
    high, low = split_np(table)
    return np.block([[high, low], [high, np.zeros_like(low)]])


def split(value):
    high = value.astype(BF16)
    return high, (value - high.astype(F32)).astype(BF16)


def dot(lhs, rhs, lhs_dim, rhs_dim):
    return lax.dot_general(
        lhs, rhs, (((lhs_dim,), (rhs_dim,)), ((), ())), preferred_element_type=F32
    )


def dot3(lhs, rhs, lhs_dim, rhs_dim):
    return (
        dot(lhs[0], rhs[0], lhs_dim, rhs_dim)
        + dot(lhs[0], rhs[1], lhs_dim, rhs_dim)
        + dot(lhs[1], rhs[0], lhs_dim, rhs_dim)
    )


def dot_paired(lhs, table):
    both = dot(jnp.concatenate(split(lhs), 1), table, 1, 0)
    return both[:, :LANES] + both[:, LANES:]


def modulo(value, count):
    if count & (count - 1) == 0:
        return value & (count - 1)
    return lax.rem(value, count)


def divide(value, count):
    if count & (count - 1) == 0:
        return lax.shift_right_logical(value, count.bit_length() - 1)
    return lax.div(value, count)


def wave_tables(cells_x):
    rows = cells_x // LANES
    k = np.arange(KMAX)
    alpha = 2 * np.pi * ((np.arange(rows)[:, None] * LANES * k) % cells_x) / cells_x
    phi = 2 * np.pi * ((np.arange(LANES)[:, None] * k) % cells_x) / cells_x
    ca, sa, cp, sp = np.cos(alpha), np.sin(alpha), np.cos(phi), np.sin(phi)
    forward = np.concatenate([ca, sa, -sa, ca], 1)
    forward_fine = np.concatenate([cp, cp, sp, sp], 1)
    inverse = np.concatenate([ca, ca, sa, sa], 1)
    inverse_fine = np.concatenate([cp, sp, cp, sp], 1)
    fine = np.stack([paired(forward_fine), paired(inverse_fine.T)])
    coarse = np.stack([forward, inverse]).astype(np.float32)
    return (jnp.asarray(coarse), jnp.asarray(fine))


def plane_tables(count_gy, count_gz, depth):
    length_y, length_z = count_gy, count_gz * depth
    waves_y, waves_z = min(KMAX, length_y), min(KMAX, length_z)
    device = np.arange(count_gy * count_gz)
    y = np.tile(device // count_gz, depth)
    z = np.concatenate([(device % count_gz) * depth + s for s in range(depth)])
    q = np.arange(waves_y * waves_z)
    phase = (y[:, None] * (q // waves_z) % length_y) / length_y
    phase = phase + (z[:, None] * (q % waves_z) % length_z) / length_z
    cos, sin = np.cos(2 * np.pi * phase), np.sin(2 * np.pi * phase)
    by_source = np.concatenate([cos, sin], 1)
    by_wave = np.concatenate([cos.T, sin.T], 1)
    return (jnp.asarray(split_np(by_source)), jnp.asarray(split_np(by_wave)))


def roll_x(value, shift, lane):
    rows = value.shape[0]
    if shift == 1:
        moved = pltpu.roll(value, 1, 1)
        return jnp.where(lane == 0, pltpu.roll(moved, 1, 0), moved)
    moved = pltpu.roll(value, LANES - 1, 1)
    return jnp.where(lane == LANES - 1, pltpu.roll(moved, rows - 1, 0), moved)


def populations(m, lane):
    rho, jx, jy, jz, pxx, pyy, pzz, pxy, pxz, pyz = m
    trace = 1.5 * (pxx + pyy + pzz)
    out = {(0, 0, 0): (2.5 * rho - trace) * (1.0 / 3.0)}
    base = rho - trace
    j = (jx, jy, jz)
    diag = (4.5 * pxx, 4.5 * pyy, 4.5 * pzz)
    for a in range(3):
        even = (base + diag[a]) * (1.0 / 18.0)
        odd = j[a] * (1.0 / 6.0)
        e = [0, 0, 0]
        e[a] = 1
        out[tuple(e)] = even + odd
        e[a] = -1
        out[tuple(e)] = even - odd
    base = -0.5 * rho - trace
    for a, b, cross in ((0, 1, pxy), (0, 2, pxz), (1, 2, pyz)):
        even = (base + (diag[a] + diag[b])) * (1.0 / 36.0)
        quarter = 0.25 * cross
        plus, minus = even + quarter, even - quarter
        total, diff = (j[a] + j[b]) * (1.0 / 12.0), (j[a] - j[b]) * (1.0 / 12.0)
        for sa, sb, value in (
            (1, 1, plus + total),
            (-1, -1, plus - total),
            (1, -1, minus + diff),
            (-1, 1, minus - diff),
        ):
            e = [0, 0, 0]
            e[a], e[b] = sa, sb
            out[tuple(e)] = value
    return {e: (roll_x(v, e[0], lane) if e[0] else v) for e, v in out.items()}


def local_totals(same, inner, e_in):
    s0, d0 = same[1] + same[-1], same[1] - same[-1]
    s1, d1 = inner[1] + inner[-1], inner[1] - inner[-1]
    layer = inner[0] + s1
    return (same[0] + s0 + layer, d0 + d1, e_in * layer, s0 + s1, layer, e_in * d1)


def early_totals(local, y, z, d, e_in):
    (s_up, x_up, e_up), (s_down, x_down, e_down) = y
    s_z, x_z = z
    up, down = s_up + d[0], s_down + d[1]
    crossing = s_z + (d[0] + d[1])
    within = e_up + e_down
    rho = local[0] + (up + down) + s_z
    jx = local[1] + (x_up + x_down) + x_z
    jy = up - down
    jz = local[2] + e_in * (within - crossing)
    pyy = up + down
    pzz = local[4] + (within + crossing)
    pxy = x_up - x_down
    pxz = local[5] - e_in * x_z
    pyz = e_in * ((e_up - e_down) - (d[0] - d[1]))
    return [rho, jx, jy, jz, None, pyy, pzz, pxy, pxz, pyz]


PAIR_LIST = ((0, 0), (1, 1), (2, 2), (0, 1), (0, 2), (1, 2))


def collide(totals, force, inverse):
    density = totals[0]
    shifted = [(totals[1 + a] + 0.5 * force[a]) * inverse for a in range(3)]
    result = [density] + [totals[1 + a] + force[a] for a in range(3)]
    third = density * (1.0 / 3.0)
    for index, (a, b) in enumerate(PAIR_LIST):
        equilibrium = density * shifted[a] * shifted[b]
        if a == b:
            equilibrium = equilibrium + third
        result.append(
            RELAX_RATE * equilibrium + (1.0 - RELAX_RATE) * totals[4 + index]
        )
    return result


def kernel(
    count_gy, count_gz, gain_scale, normalizer,
    moments_in, wavenumbers_in, gain_in, coarse_in, fine_in, source_in, wave_in,
    final, coeffs,
    moments, wavenumbers, gain, coarse_tables, fine, source_tables, wave_tables_ref,
    load, gathered, filters, send_early, send_late, recv_early, recv_late,
    gather_send, gather_recv, early_sems, late_sems,
):
    depth, rows = moments.shape[1:3]
    devices = count_gy * count_gz
    my_y, my_z = lax.axis_index("gy"), lax.axis_index("gz")
    me = my_y * count_gz + my_z
    lane = lax.broadcasted_iota(jnp.int32, (rows, LANES), 1)
    lane1 = lax.broadcasted_iota(jnp.int32, (1, LANES), 1)

    def peer(i):
        if devices & (devices - 1) == 0:
            target = me ^ i
        else:
            target = modulo(me + i, devices)
        return (divide(target, count_gz), modulo(target, count_gz))

    barrier = pltpu.get_barrier_semaphore()

    def greet(i, carry):
        pl.semaphore_signal(barrier, inc=1, device_id=peer(devices - i), device_id_type=MESH)
        return carry

    lax.fori_loop(1, devices, greet, 0)

    loads = [
        pltpu.make_async_copy(src, dst, load.at[i])
        for i, (src, dst) in enumerate((
            (moments_in, moments), (coarse_in, coarse_tables), (fine_in, fine),
            (wavenumbers_in, wavenumbers), (gain_in, gain), (source_in, source_tables),
            (wave_in, wave_tables_ref),
        ))
    ]
    for copy in loads:
        copy.start()

    def y_at(step):
        return modulo(my_y + step + count_gy, count_gy)

    def z_at(step):
        return modulo(my_z + step + count_gz, count_gz)

    def halo(step, src, dst, sems, start, count, dy, dz):
        pltpu.make_async_remote_copy(
            src_ref=src.at[step, pl.ds(start, count)], dst_ref=dst.at[step, pl.ds(start, count)],
            send_sem=sems.at[0, step], recv_sem=sems.at[1, step],
            device_id=(y_at(dy), z_at(dz)), device_id_type=MESH,
        ).start()

    def send_halo_early(step):
        def copy(start, count, dy, dz):
            halo(step, send_early, recv_early, early_sems, start, count, dy, dz)

        if count_gz == 2:
            copy(16, 2, 1, 1)
            copy(18, 2, -1, 1)
        else:
            copy(16, 1, 1, 1)
            copy(17, 1, 1, -1)
            copy(18, 1, -1, 1)
            copy(19, 1, -1, -1)
        copy(0, 6, 1, 0)
        copy(6, 6, -1, 0)
        if count_gz == 2:
            copy(12, 4, 0, 1)
        else:
            copy(12, 2, 0, 1)
            copy(14, 2, 0, -1)

    def send_halo_late(step):
        def copy(start, count, dy, dz):
            halo(step, send_late, recv_late, late_sems, start, count, dy, dz)

        copy(0, 2, 1, 0)
        copy(2, 2, -1, 0)
        if count_gz == 2:
            copy(4, 2, 0, 1)
        else:
            copy(4, 1, 0, 1)
            copy(5, 1, 0, -1)

    def send_gather(step):
        def send(i, carry):
            pltpu.make_async_remote_copy(
                src_ref=gathered.at[step, me], dst_ref=gathered.at[step, me],
                send_sem=gather_send.at[step], recv_sem=gather_recv.at[step],
                device_id=peer(devices - i), device_id_type=MESH,
            ).start()
            return carry

        lax.fori_loop(1, devices, send, 0)

    def wait_for(ref, sem):
        pltpu.make_async_copy(ref, ref, sem).wait()

    waves_y, waves_z = min(KMAX, count_gy), min(KMAX, count_gz * depth)
    modes = wavenumbers.shape[1]

    def wave_onehot():
        q = modulo(wavenumbers[1:2, :], count_gy) * waves_z
        q = q + modulo(wavenumbers[2:3, :], count_gz * depth)
        index = lax.broadcasted_iota(jnp.int32, (waves_y * waves_z, modes), 0)
        return jnp.where(index == q, 1.0, 0.0)

    def x_onehot():
        index = lax.broadcasted_iota(jnp.int32, (KMAX, modes), 0)
        return jnp.where(index == wavenumbers[0:1, :], 1.0, 0.0)

    def build_filters():
        count_q = waves_y * waves_z
        onehot_q = wave_onehot()
        weighted = split(onehot_q * gain[...])
        onehot_x = x_onehot().astype(BF16)
        onehot_x = jnp.concatenate([onehot_x] * 4, 0)
        energy = dot(weighted[0], onehot_x, 1, 1) + dot(weighted[1], onehot_x, 1, 1)
        energy = energy * gain_scale
        index = lax.broadcasted_iota(jnp.int32, (count_q, LANES), 0)
        wave_y, wave_z = divide(index, waves_z), modulo(index, waves_z)
        length_z = count_gz * depth
        phase_y = modulo(wave_y * my_y, count_gy).astype(F32) * (1.0 / count_gy)
        for t in range(depth):
            phase = modulo(wave_z * (my_z * depth + t), length_z).astype(F32)
            angle = (2.0 * math.pi) * (phase_y + phase * (1.0 / length_z))
            ec, es = energy * jnp.cos(angle), energy * jnp.sin(angle)
            for part, stack in enumerate(((ec, es), (es, -ec))):
                pieces = split(jnp.concatenate(stack, 0))
                table = dot3((source_tables[0], source_tables[1]), pieces, 1, 0)
                filters[2 * t + part] = jnp.where(
                    lane1 < LANES // 2, table[:devices], table[devices:]
                )

    def store_coeffs(spectra):
        half = LANES // 2
        sign = jnp.where((lane1 & KMAX) == 0, -1.0, 1.0)
        blocks = []
        for a in range(3):
            top = jnp.concatenate([spectra[a], pltpu.roll(spectra[a], half, 1)], 0)
            swapped = jnp.where((lane1 & KMAX) == 0, pltpu.roll(top, LANES - KMAX, 1), pltpu.roll(top, KMAX, 1))
            blocks.append(jnp.concatenate([top, sign * swapped], 0)[:, :half])
        stacked = jnp.concatenate(blocks, 1)
        transform = dot3((wave_tables_ref[0], wave_tables_ref[1]), split(stacked), 1, 0) * normalizer
        pieces = split(transform)
        onehot_q = wave_onehot().astype(BF16)
        chosen = dot(pieces[0], onehot_q, 0, 0) + dot(pieces[1], onehot_q, 0, 0)
        onehot_x = x_onehot()
        for a in range(3):
            for part in range(2):
                start = (2 * a + part) * KMAX
                picked = jnp.sum(chosen[start : start + KMAX] * onehot_x, axis=0, keepdims=True)
                coeffs[a, part : part + 1, :] = picked

    def project(step, speed):
        stacked = jnp.concatenate([speed[z][a] for z in range(depth) for a in range(3)], 0)
        coarse = dot_paired(stacked, fine[0])
        table = coarse_tables[0]
        folded = []
        for r in range(3 * depth):
            part = jnp.sum(coarse[r * rows : (r + 1) * rows] * table, axis=0, keepdims=True)
            folded.append(part + pltpu.roll(part, LANES // 2, 1))
        for a in range(3):
            packed = jnp.where(lane1 < LANES // 2, folded[a], folded[3 + a])
            gathered[step, me, :, a * LANES : (a + 1) * LANES] = packed

    def make_force(spectra):
        inverse_coarse = coarse_tables[1]
        swap_sign = jnp.where((lane1 & KMAX) == 0, 1.0, -1.0)
        outer_sign = jnp.where(lane1 < 3 * KMAX, 1.0, -1.0)
        expanded = []
        for z in range(depth):
            for a in range(3):
                first = jnp.sum(spectra[a] * filters[2 * z], axis=0, keepdims=True)
                second = jnp.sum(spectra[a] * filters[2 * z + 1], axis=0, keepdims=True)
                first = first + pltpu.roll(first, LANES // 2, 1)
                second = second + pltpu.roll(second, LANES // 2, 1)
                both = first + swap_sign * pltpu.roll(second, KMAX, 1)
                row = jnp.where(
                    lane1 < LANES // 2, both, outer_sign * pltpu.roll(both, KMAX, 1)
                )
                expanded.append(inverse_coarse * row)
        force = dot_paired(jnp.concatenate(expanded, 0), fine[1])
        return [
            [force[(3 * z + a) * rows : (3 * z + a + 1) * rows] for a in range(3)]
            for z in range(depth)
        ]

    inside = (-1, 1)

    def stage_halo(step, pops):
        for z in range(2):
            e_in, other = inside[z], pops[1 - z]
            for i, sy in enumerate((1, -1)):
                plus, minus = pops[z][1, sy, 0], pops[z][-1, sy, 0]
                both, crossing = plus + minus, other[0, sy, e_in]
                row = 6 * i + 3 * z
                send_early[step, row] = (pops[z][0, sy, 0] + both) + crossing
                send_early[step, row + 1] = plus - minus
                send_early[step, row + 2] = crossing
                send_early[step, 16 + 2 * i + z] = other[0, sy, -e_in]
                send_late[step, 2 * i + z] = both
            plus, minus = other[1, 0, -e_in], other[-1, 0, -e_in]
            both = plus + minus
            send_early[step, 12 + 2 * z] = other[0, 0, -e_in] + both
            send_early[step, 13 + 2 * z] = plus - minus
            send_late[step, 4 + z] = both

    def own_totals(pops):
        out = []
        for z in range(2):
            same = {sx: pops[z][sx, 0, 0] for sx in (0, 1, -1)}
            inner = {sx: pops[1 - z][sx, 0, inside[z]] for sx in (0, 1, -1)}
            out.append(local_totals(same, inner, float(inside[z])))
        return out

    def speeds(layers, inverse):
        return [[layers[z][1 + a] * inverse[z] for a in range(3)] for z in range(depth)]

    for copy in loads[:3]:
        copy.wait()
    layers = [[moments[i, z] for i in range(10)] for z in range(depth)]
    project(0, speeds(layers, [1.0 / layers[z][0] for z in range(depth)]))
    pl.semaphore_wait(barrier, devices - 1)
    send_gather(0)
    pops = [populations(layers[z], lane) for z in range(depth)]
    stage_halo(0, pops)
    send_halo_early(0)
    send_halo_late(0)
    for copy in loads[3:]:
        copy.wait()
    build_filters()

    for step in range(STEPS):
        last = step == STEPS - 1
        local = own_totals(pops)
        wait_for(gathered.at[step, pl.ds(0, devices - 1)], gather_recv.at[step])
        spectra = [gathered[step, :, 0, a * LANES : (a + 1) * LANES] for a in range(3)]
        force = make_force(spectra)
        if last:
            store_coeffs(spectra)
        wait_for(recv_early.at[step], early_sems.at[1, step])
        totals, inverse = [], []
        for z in range(depth):
            y = [[recv_early[step, 6 * i + 3 * z + n] for n in range(3)] for i in range(2)]
            totals.append(
                early_totals(
                    local[z], y, [recv_early[step, 12 + 2 * z + n] for n in range(2)],
                    [recv_early[step, 16 + 2 * i + z] for i in range(2)], float(inside[z]),
                )
            )
            inverse.append(1.0 / totals[z][0])
        if not last:
            moved = [
                [None] + [totals[z][1 + a] + force[z][a] for a in range(3)] for z in range(depth)
            ]
            project(step + 1, speeds(moved, inverse))
            send_gather(step + 1)
        wait_for(recv_late.at[step], late_sems.at[1, step])
        results = []
        for z in range(depth):
            totals[z][4] = local[z][3] + (
                (recv_late[step, z] + recv_late[step, 2 + z]) + recv_late[step, 4 + z]
            )
            results.append(collide(totals[z], force[z], inverse[z]))
        if last:
            for z in range(depth):
                for i in range(10):
                    final[i, z] = results[z][i]
        else:
            pops = [populations(results[z], lane) for z in range(depth)]
            stage_halo(step + 1, pops)
            send_halo_early(step + 1)
            send_halo_late(step + 1)

    for step in range(STEPS):
        wait_for(gathered.at[step, pl.ds(0, devices - 1)], gather_send.at[step])
        wait_for(send_early.at[step], early_sems.at[0, step])
        wait_for(send_late.at[step], late_sems.at[0, step])


def hand_over(final_in, coeffs_in, final_out, coeffs_out, sems):
    copies = [
        pltpu.make_async_copy(final_in, final_out, sems.at[0]),
        pltpu.make_async_copy(coeffs_in, coeffs_out, sems.at[1]),
    ]
    for copy in copies:
        copy.start()
    for copy in copies:
        copy.wait()


def per_device(count_gy, count_gz, moments, wavenumbers, mode_gain):
    depth, height, cells_x = moments.shape[1:]
    assert height == 1 and depth == 2 and cells_x % 1024 == 0
    rows = cells_x // LANES
    modes = mode_gain.shape[0]
    devices = count_gy * count_gz
    normalizer = 1.0 / math.sqrt(cells_x * height * depth * devices)
    force_scale = FORCE_GAIN / math.sqrt(2 * modes * devices)
    tables = wave_tables(cells_x) + plane_tables(count_gy, count_gz, depth)
    operands = (moments.reshape(10, depth, rows, LANES), wavenumbers, mode_gain.reshape(1, modes)) + tables
    vmem = pl.BlockSpec(memory_space=pltpu.VMEM)
    final, coeffs = pl.pallas_call(
        functools.partial(kernel, count_gy, count_gz, force_scale * normalizer, normalizer),
        out_shape=(
            pltpu.VMEM((10, depth, rows, LANES), F32),
            pltpu.VMEM((3, 2, modes), F32),
        ),
        in_specs=[pl.BlockSpec(memory_space=pl.ANY)] * len(operands),
        out_specs=(vmem, vmem),
        scratch_shapes=[pltpu.VMEM(x.shape, x.dtype) for x in operands] + [
            pltpu.SemaphoreType.DMA((len(operands),)),
            pltpu.VMEM((STEPS, devices, 1, 3 * LANES), F32),
            pltpu.VMEM((2 * depth, devices, LANES), F32),
            pltpu.VMEM((STEPS, 20, rows, LANES), F32),
            pltpu.VMEM((STEPS, 6, rows, LANES), F32),
            pltpu.VMEM((STEPS, 20, rows, LANES), F32),
            pltpu.VMEM((STEPS, 6, rows, LANES), F32),
            pltpu.SemaphoreType.DMA((STEPS,)),
            pltpu.SemaphoreType.DMA((STEPS,)),
            pltpu.SemaphoreType.DMA((2, STEPS)),
            pltpu.SemaphoreType.DMA((2, STEPS)),
        ],
        compiler_params=pltpu.CompilerParams(
            collective_id=0, has_side_effects=True, vmem_limit_bytes=60 * 1024 * 1024
        ),
    )(*operands)
    final, coeffs = pl.pallas_call(
        hand_over,
        out_shape=(
            jax.ShapeDtypeStruct(final.shape, F32),
            jax.ShapeDtypeStruct(coeffs.shape, F32),
        ),
        in_specs=[vmem] * 2,
        out_specs=(pl.BlockSpec(memory_space=pl.ANY), pl.BlockSpec(memory_space=pl.ANY)),
        scratch_shapes=[pltpu.SemaphoreType.DMA((2,))],
        compiler_params=pltpu.CompilerParams(vmem_limit_bytes=4 * 1024 * 1024),
    )(final, coeffs)
    return final.reshape(moments.shape), jnp.transpose(coeffs, (1, 0, 2))


def solution(mesh):
    in_specs = (P(None, "gz", "gy", None), P(), P())
    out_specs = (P(None, "gz", "gy", None), P())
    body = functools.partial(per_device, mesh.shape["gy"], mesh.shape["gz"])
    return jax.shard_map(
        body, mesh=mesh, in_specs=in_specs, out_specs=out_specs, check_vma=False
    )
```

```python
import functools
import math

import jax
import jax.numpy as jnp
import numpy as np
from jax import lax
from jax.experimental import pallas as pl
from jax.experimental.pallas import tpu as pltpu
from jax.sharding import PartitionSpec as P

KMAX = 32
STEPS = 3
RELAX_RATE = 1.6
FORCE_GAIN = 0.5
LANES = 128
MESH = pl.DeviceIdType.MESH
F32 = jnp.float32
BF16 = jnp.bfloat16


def split_np(table):
    high = table.astype(np.float32).astype(jnp.bfloat16)
    low = (table.astype(np.float32) - high.astype(np.float32)).astype(jnp.bfloat16)
    return np.stack([high, low])


def paired(table):
    high, low = split_np(table)
    return np.block([[high, low], [high, np.zeros_like(low)]])


def split(value):
    high = value.astype(BF16)
    return high, (value - high.astype(F32)).astype(BF16)


def dot(lhs, rhs, lhs_dim, rhs_dim):
    return lax.dot_general(
        lhs, rhs, (((lhs_dim,), (rhs_dim,)), ((), ())), preferred_element_type=F32
    )


def dot3(lhs, rhs, lhs_dim, rhs_dim):
    return (
        dot(lhs[0], rhs[0], lhs_dim, rhs_dim)
        + dot(lhs[0], rhs[1], lhs_dim, rhs_dim)
        + dot(lhs[1], rhs[0], lhs_dim, rhs_dim)
    )


def dot_paired(lhs, table):
    both = dot(jnp.concatenate(split(lhs), 1), table, 1, 0)
    return both[:, :LANES] + both[:, LANES:]


def modulo(value, count):
    if count & (count - 1) == 0:
        return value & (count - 1)
    return lax.rem(value, count)


def divide(value, count):
    if count & (count - 1) == 0:
        return lax.shift_right_logical(value, count.bit_length() - 1)
    return lax.div(value, count)


def wave_tables(cells_x):
    rows = cells_x // LANES
    k = np.arange(KMAX)
    alpha = 2 * np.pi * ((np.arange(rows)[:, None] * LANES * k) % cells_x) / cells_x
    phi = 2 * np.pi * ((np.arange(LANES)[:, None] * k) % cells_x) / cells_x
    ca, sa, cp, sp = np.cos(alpha), np.sin(alpha), np.cos(phi), np.sin(phi)
    forward = np.concatenate([ca, sa, -sa, ca], 1)
    forward_fine = np.concatenate([cp, cp, sp, sp], 1)
    inverse = np.concatenate([ca, ca, sa, sa], 1)
    inverse_fine = np.concatenate([cp, sp, cp, sp], 1)
    fine = np.stack([paired(forward_fine), paired(inverse_fine.T)])
    coarse = np.stack([forward, inverse]).astype(np.float32)
    return (jnp.asarray(coarse), jnp.asarray(fine))


def plane_tables(count_gy, count_gz, depth):
    length_y, length_z = count_gy, count_gz * depth
    waves_y, waves_z = min(KMAX, length_y), min(KMAX, length_z)
    device = np.arange(count_gy * count_gz)
    y = np.tile(device // count_gz, depth)
    z = np.concatenate([(device % count_gz) * depth + s for s in range(depth)])
    q = np.arange(waves_y * waves_z)
    phase = (y[:, None] * (q // waves_z) % length_y) / length_y
    phase = phase + (z[:, None] * (q % waves_z) % length_z) / length_z
    cos, sin = np.cos(2 * np.pi * phase), np.sin(2 * np.pi * phase)
    by_source = np.concatenate([cos, sin], 1)
    by_wave = np.concatenate([cos.T, sin.T], 1)
    return (jnp.asarray(split_np(by_source)), jnp.asarray(split_np(by_wave)))


def roll_x(value, shift, lane):
    rows = value.shape[0]
    if shift == 1:
        moved = pltpu.roll(value, 1, 1)
        return jnp.where(lane == 0, pltpu.roll(moved, 1, 0), moved)
    moved = pltpu.roll(value, LANES - 1, 1)
    return jnp.where(lane == LANES - 1, pltpu.roll(moved, rows - 1, 0), moved)


def populations(m, lane):
    rho, jx, jy, jz, pxx, pyy, pzz, pxy, pxz, pyz = m
    trace = 1.5 * (pxx + pyy + pzz)
    out = {(0, 0, 0): (2.5 * rho - trace) * (1.0 / 3.0)}
    base = rho - trace
    j = (jx, jy, jz)
    diag = (4.5 * pxx, 4.5 * pyy, 4.5 * pzz)
    for a in range(3):
        even = (base + diag[a]) * (1.0 / 18.0)
        odd = j[a] * (1.0 / 6.0)
        e = [0, 0, 0]
        e[a] = 1
        out[tuple(e)] = even + odd
        e[a] = -1
        out[tuple(e)] = even - odd
    base = -0.5 * rho - trace
    for a, b, cross in ((0, 1, pxy), (0, 2, pxz), (1, 2, pyz)):
        even = (base + (diag[a] + diag[b])) * (1.0 / 36.0)
        quarter = 0.25 * cross
        plus, minus = even + quarter, even - quarter
        total, diff = (j[a] + j[b]) * (1.0 / 12.0), (j[a] - j[b]) * (1.0 / 12.0)
        for sa, sb, value in (
            (1, 1, plus + total),
            (-1, -1, plus - total),
            (1, -1, minus + diff),
            (-1, 1, minus - diff),
        ):
            e = [0, 0, 0]
            e[a], e[b] = sa, sb
            out[tuple(e)] = value
    return {e: (roll_x(v, e[0], lane) if e[0] else v) for e, v in out.items()}


def local_totals(same, inner, e_in):
    s0, d0 = same[1] + same[-1], same[1] - same[-1]
    s1, d1 = inner[1] + inner[-1], inner[1] - inner[-1]
    layer = inner[0] + s1
    return (same[0] + s0 + layer, d0 + d1, e_in * layer, s0 + s1, layer, e_in * d1)


def totals_of(local, y, z, d, e_in):
    (s_up, x_up, e_up, xx_up), (s_down, x_down, e_down, xx_down) = y
    s_z, x_z, xx_z = z
    up, down = s_up + d[0], s_down + d[1]
    crossing = s_z + (d[0] + d[1])
    within = e_up + e_down
    rho = local[0] + (up + down) + s_z
    jx = local[1] + (x_up + x_down) + x_z
    jy = up - down
    jz = local[2] + e_in * (within - crossing)
    pxx = local[3] + (xx_up + xx_down) + xx_z
    pyy = up + down
    pzz = local[4] + (within + crossing)
    pxy = x_up - x_down
    pxz = local[5] - e_in * x_z
    pyz = e_in * ((e_up - e_down) - (d[0] - d[1]))
    return [rho, jx, jy, jz, pxx, pyy, pzz, pxy, pxz, pyz]


PAIR_LIST = ((0, 0), (1, 1), (2, 2), (0, 1), (0, 2), (1, 2))


def collide(totals, force, inverse):
    density = totals[0]
    shifted = [(totals[1 + a] + 0.5 * force[a]) * inverse for a in range(3)]
    result = [density] + [totals[1 + a] + force[a] for a in range(3)]
    third = density * (1.0 / 3.0)
    for index, (a, b) in enumerate(PAIR_LIST):
        equilibrium = density * shifted[a] * shifted[b]
        if a == b:
            equilibrium = equilibrium + third
        result.append(
            RELAX_RATE * equilibrium + (1.0 - RELAX_RATE) * totals[4 + index]
        )
    return result


def kernel(
    count_gy, count_gz, gain_scale, normalizer,
    moments_in, wavenumbers_in, gain_in, coarse_in, fine_in, source_in, wave_in,
    final, coeffs,
    moments, wavenumbers, gain, coarse_tables, fine, source_tables, wave_tables_ref,
    load, gathered, filters, send_halo, recv_halo,
    gather_send, gather_recv, first_sems, rest_sems,
):
    depth, rows = moments.shape[1:3]
    devices = count_gy * count_gz
    my_y, my_z = lax.axis_index("gy"), lax.axis_index("gz")
    me = my_y * count_gz + my_z
    lane = lax.broadcasted_iota(jnp.int32, (rows, LANES), 1)
    lane1 = lax.broadcasted_iota(jnp.int32, (1, LANES), 1)

    def peer(i):
        if devices & (devices - 1) == 0:
            target = me ^ i
        else:
            target = modulo(me + i, devices)
        return (divide(target, count_gz), modulo(target, count_gz))

    barrier = pltpu.get_barrier_semaphore()

    def greet(i, carry):
        pl.semaphore_signal(barrier, inc=1, device_id=peer(devices - i), device_id_type=MESH)
        return carry

    lax.fori_loop(1, devices, greet, 0)

    loads = [
        pltpu.make_async_copy(src, dst, load.at[i])
        for i, (src, dst) in enumerate((
            (moments_in, moments), (coarse_in, coarse_tables), (fine_in, fine),
            (wavenumbers_in, wavenumbers), (gain_in, gain), (source_in, source_tables),
            (wave_in, wave_tables_ref),
        ))
    ]
    for copy in loads:
        copy.start()

    def y_at(step):
        return modulo(my_y + step + count_gy, count_gy)

    def z_at(step):
        return modulo(my_z + step + count_gz, count_gz)

    first_rows = ((0, rows - 8), (8, rows - 24), (9, rows - 26))

    def rest_rows(step):
        start, count = first_rows[step]
        spans = [(start + count, rows - start - count)]
        return spans + [(0, start)] if start else spans

    def send_rows(step, spans, sems):
        messages = [(0, 8, 1, 0), (8, 8, -1, 0)]
        if count_gz == 2:
            messages = [(22, 2, 1, 1), (24, 2, -1, 1)] + messages + [(16, 6, 0, 1)]
        else:
            messages = [
                (22, 1, 1, 1), (23, 1, 1, -1), (24, 1, -1, 1), (25, 1, -1, -1)
            ] + messages + [(16, 3, 0, 1), (19, 3, 0, -1)]
        for start, count in spans:
            for kind, kinds, dy, dz in messages:
                part = (step, pl.ds(kind, kinds), pl.ds(start, count))
                pltpu.make_async_remote_copy(
                    src_ref=send_halo.at[part], dst_ref=recv_halo.at[part],
                    send_sem=sems.at[0, step], recv_sem=sems.at[1, step],
                    device_id=(y_at(dy), z_at(dz)), device_id_type=MESH,
                ).start()

    def wait_rows(step, ref, count, sem):
        part = ref.at[step, :, pl.ds(0, count)]
        pltpu.make_async_copy(part, part, sem).wait()

    def wait_first(step, ref, side):
        wait_rows(step, ref, first_rows[step][1], first_sems.at[side, step])

    def wait_rest(step, ref, side):
        wait_rows(step, ref, rows - first_rows[step][1], rest_sems.at[side, step])

    def send_gather(step):
        def send(i, carry):
            pltpu.make_async_remote_copy(
                src_ref=gathered.at[step, me], dst_ref=gathered.at[step, me],
                send_sem=gather_send.at[step], recv_sem=gather_recv.at[step],
                device_id=peer(devices - i), device_id_type=MESH,
            ).start()
            return carry

        if devices <= 32:
            for i in range(1, devices):
                send(i, 0)
        else:
            lax.fori_loop(1, devices, send, 0)

    def wait_for(ref, sem):
        pltpu.make_async_copy(ref, ref, sem).wait()

    waves_y, waves_z = min(KMAX, count_gy), min(KMAX, count_gz * depth)
    modes = wavenumbers.shape[1]

    def wave_onehot():
        q = modulo(wavenumbers[1:2, :], count_gy) * waves_z
        q = q + modulo(wavenumbers[2:3, :], count_gz * depth)
        index = lax.broadcasted_iota(jnp.int32, (waves_y * waves_z, modes), 0)
        return jnp.where(index == q, 1.0, 0.0)

    def x_onehot():
        index = lax.broadcasted_iota(jnp.int32, (KMAX, modes), 0)
        return jnp.where(index == wavenumbers[0:1, :], 1.0, 0.0)

    def build_filters():
        count_q = waves_y * waves_z
        onehot_q = wave_onehot()
        weighted = split(onehot_q * gain[...])
        onehot_x = x_onehot().astype(BF16)
        onehot_x = jnp.concatenate([onehot_x] * 4, 0)
        energy = dot(weighted[0], onehot_x, 1, 1) + dot(weighted[1], onehot_x, 1, 1)
        energy = energy * gain_scale
        index = lax.broadcasted_iota(jnp.int32, (count_q, LANES), 0)
        wave_y, wave_z = divide(index, waves_z), modulo(index, waves_z)
        length_z = count_gz * depth
        phase_y = modulo(wave_y * my_y, count_gy).astype(F32) * (1.0 / count_gy)
        for t in range(depth):
            phase = modulo(wave_z * (my_z * depth + t), length_z).astype(F32)
            angle = (2.0 * math.pi) * (phase_y + phase * (1.0 / length_z))
            ec, es = energy * jnp.cos(angle), energy * jnp.sin(angle)
            for part, stack in enumerate(((ec, es), (es, -ec))):
                pieces = split(jnp.concatenate(stack, 0))
                table = dot3((source_tables[0], source_tables[1]), pieces, 1, 0)
                filters[2 * t + part] = jnp.where(
                    lane1 < LANES // 2, table[:devices], table[devices:]
                )

    def store_coeffs(spectra):
        half = LANES // 2
        sign = jnp.where((lane1 & KMAX) == 0, -1.0, 1.0)
        blocks = []
        for a in range(3):
            top = jnp.concatenate([spectra[a], pltpu.roll(spectra[a], half, 1)], 0)
            swapped = jnp.where((lane1 & KMAX) == 0, pltpu.roll(top, LANES - KMAX, 1), pltpu.roll(top, KMAX, 1))
            blocks.append(jnp.concatenate([top, sign * swapped], 0)[:, :half])
        stacked = jnp.concatenate(blocks, 1)
        transform = dot3((wave_tables_ref[0], wave_tables_ref[1]), split(stacked), 1, 0) * normalizer
        pieces = split(transform)
        onehot_q = wave_onehot().astype(BF16)
        chosen = dot(pieces[0], onehot_q, 0, 0) + dot(pieces[1], onehot_q, 0, 0)
        onehot_x = x_onehot()
        for a in range(3):
            for part in range(2):
                start = (2 * a + part) * KMAX
                picked = jnp.sum(chosen[start : start + KMAX] * onehot_x, axis=0, keepdims=True)
                coeffs[a, part : part + 1, :] = picked

    def project(step, speed):
        stacked = jnp.concatenate([speed[z][a] for z in range(depth) for a in range(3)], 0)
        coarse = dot_paired(stacked, fine[0])
        table = coarse_tables[0]
        folded = []
        for r in range(3 * depth):
            part = jnp.sum(coarse[r * rows : (r + 1) * rows] * table, axis=0, keepdims=True)
            folded.append(part + pltpu.roll(part, LANES // 2, 1))
        for a in range(3):
            packed = jnp.where(lane1 < LANES // 2, folded[a], folded[3 + a])
            gathered[step, me, :, a * LANES : (a + 1) * LANES] = packed

    def make_force(spectra):
        inverse_coarse = coarse_tables[1]
        swap_sign = jnp.where((lane1 & KMAX) == 0, 1.0, -1.0)
        outer_sign = jnp.where(lane1 < 3 * KMAX, 1.0, -1.0)
        expanded = []
        for z in range(depth):
            for a in range(3):
                first = jnp.sum(spectra[a] * filters[2 * z], axis=0, keepdims=True)
                second = jnp.sum(spectra[a] * filters[2 * z + 1], axis=0, keepdims=True)
                first = first + pltpu.roll(first, LANES // 2, 1)
                second = second + pltpu.roll(second, LANES // 2, 1)
                both = first + swap_sign * pltpu.roll(second, KMAX, 1)
                row = jnp.where(
                    lane1 < LANES // 2, both, outer_sign * pltpu.roll(both, KMAX, 1)
                )
                expanded.append(inverse_coarse * row)
        force = dot_paired(jnp.concatenate(expanded, 0), fine[1])
        return [
            [force[(3 * z + a) * rows : (3 * z + a + 1) * rows] for a in range(3)]
            for z in range(depth)
        ]

    inside = (-1, 1)

    def stage_halo(step, pops, spans, base=0):
        def put(kind, value):
            for start, count in spans:
                send_halo[step, kind, start : start + count] = value[
                    start - base : start - base + count
                ]

        for z in range(2):
            e_in, other = inside[z], pops[1 - z]
            for i, sy in enumerate((1, -1)):
                plus, minus = pops[z][1, sy, 0], pops[z][-1, sy, 0]
                both, crossing = plus + minus, other[0, sy, e_in]
                kind = 8 * i + 4 * z
                put(kind, (pops[z][0, sy, 0] + both) + crossing)
                put(kind + 1, plus - minus)
                put(kind + 2, crossing)
                put(kind + 3, both)
                put(22 + 2 * i + z, other[0, sy, -e_in])
            plus, minus = other[1, 0, -e_in], other[-1, 0, -e_in]
            both = plus + minus
            put(16 + 3 * z, other[0, 0, -e_in] + both)
            put(17 + 3 * z, plus - minus)
            put(18 + 3 * z, both)

    def stream(step, local, start, count):
        span = slice(start, start + count)
        totals = []
        for z in range(depth):
            y = [[recv_halo[step, 8 * i + 4 * z + n, span] for n in range(4)] for i in range(2)]
            totals.append(
                totals_of(
                    [value[span] for value in local[z]], y,
                    [recv_halo[step, 16 + 3 * z + n, span] for n in range(3)],
                    [recv_halo[step, 22 + 2 * i + z, span] for i in range(2)], float(inside[z]),
                )
            )
        return totals, [1.0 / totals[z][0] for z in range(depth)]

    def own_totals(pops):
        out = []
        for z in range(2):
            same = {sx: pops[z][sx, 0, 0] for sx in (0, 1, -1)}
            inner = {sx: pops[1 - z][sx, 0, inside[z]] for sx in (0, 1, -1)}
            out.append(local_totals(same, inner, float(inside[z])))
        return out

    def speeds(layers, inverse):
        return [[layers[z][1 + a] * inverse[z] for a in range(3)] for z in range(depth)]

    for copy in loads[:3]:
        copy.wait()
    layers = [[moments[i, z] for i in range(10)] for z in range(depth)]
    project(0, speeds(layers, [1.0 / layers[z][0] for z in range(depth)]))
    pl.semaphore_wait(barrier, devices - 1)
    send_gather(0)
    pops = [populations(layers[z], lane) for z in range(depth)]
    stage_halo(0, pops, [(0, rows)])
    send_rows(0, [first_rows[0]], first_sems)
    send_rows(0, rest_rows(0), rest_sems)
    for copy in loads[3:]:
        copy.wait()
    build_filters()

    for step in range(STEPS):
        last = step == STEPS - 1
        local = own_totals(pops)
        wait_for(gathered.at[step, pl.ds(0, devices - 1)], gather_recv.at[step])
        spectra = [gathered[step, :, 0, a * LANES : (a + 1) * LANES] for a in range(3)]
        force = make_force(spectra)
        if last:
            store_coeffs(spectra)
        wait_first(step, recv_halo, 1)
        if not last:
            start, count = (0, rows - 8) if step == 0 else (8, rows - 24)
            totals, inverse = stream(step, local, start, count)
            piece = [[value[start : start + count] for value in force[z]] for z in range(depth)]
            ahead = [collide(totals[z], piece[z], inverse[z]) for z in range(depth)]
            ahead = [populations(ahead[z], lane[:count]) for z in range(depth)]
            stage_halo(step + 1, ahead, [first_rows[step + 1]], start)
            send_rows(step + 1, [first_rows[step + 1]], first_sems)
        wait_rest(step, recv_halo, 1)
        totals, inverse = stream(step, local, 0, rows)
        if not last:
            moved = [
                [None] + [totals[z][1 + a] + force[z][a] for a in range(3)] for z in range(depth)
            ]
            project(step + 1, speeds(moved, inverse))
            send_gather(step + 1)
        results = [collide(totals[z], force[z], inverse[z]) for z in range(depth)]
        if last:
            for z in range(depth):
                for i in range(10):
                    final[i, z] = results[z][i]
        else:
            pops = [populations(results[z], lane) for z in range(depth)]
            stage_halo(step + 1, pops, rest_rows(step + 1))
            send_rows(step + 1, rest_rows(step + 1), rest_sems)

    for step in range(STEPS):
        wait_for(gathered.at[step, pl.ds(0, devices - 1)], gather_send.at[step])
        wait_first(step, send_halo, 0)
        wait_rest(step, send_halo, 0)


def hand_over(final_in, coeffs_in, final_out, coeffs_out, sems):
    copies = [
        pltpu.make_async_copy(final_in, final_out, sems.at[0]),
        pltpu.make_async_copy(coeffs_in, coeffs_out, sems.at[1]),
    ]
    for copy in copies:
        copy.start()
    for copy in copies:
        copy.wait()


def per_device(count_gy, count_gz, moments, wavenumbers, mode_gain):
    depth, height, cells_x = moments.shape[1:]
    assert height == 1 and depth == 2 and cells_x % 1024 == 0 and cells_x >= 4096
    rows = cells_x // LANES
    modes = mode_gain.shape[0]
    devices = count_gy * count_gz
    normalizer = 1.0 / math.sqrt(cells_x * height * depth * devices)
    force_scale = FORCE_GAIN / math.sqrt(2 * modes * devices)
    tables = wave_tables(cells_x) + plane_tables(count_gy, count_gz, depth)
    operands = (moments.reshape(10, depth, rows, LANES), wavenumbers, mode_gain.reshape(1, modes)) + tables
    vmem = pl.BlockSpec(memory_space=pltpu.VMEM)
    final, coeffs = pl.pallas_call(
        functools.partial(kernel, count_gy, count_gz, force_scale * normalizer, normalizer),
        out_shape=(
            pltpu.VMEM((10, depth, rows, LANES), F32),
            pltpu.VMEM((3, 2, modes), F32),
        ),
        in_specs=[pl.BlockSpec(memory_space=pl.ANY)] * len(operands),
        out_specs=(vmem, vmem),
        scratch_shapes=[pltpu.VMEM(x.shape, x.dtype) for x in operands] + [
            pltpu.SemaphoreType.DMA((len(operands),)),
            pltpu.VMEM((STEPS, devices, 1, 3 * LANES), F32),
            pltpu.VMEM((2 * depth, devices, LANES), F32),
            pltpu.VMEM((STEPS, 26, rows, LANES), F32),
            pltpu.VMEM((STEPS, 26, rows, LANES), F32),
            pltpu.SemaphoreType.DMA((STEPS,)),
            pltpu.SemaphoreType.DMA((STEPS,)),
            pltpu.SemaphoreType.DMA((2, STEPS)),
            pltpu.SemaphoreType.DMA((2, STEPS)),
        ],
        compiler_params=pltpu.CompilerParams(
            collective_id=0, has_side_effects=True, vmem_limit_bytes=60 * 1024 * 1024
        ),
    )(*operands)
    final, coeffs = pl.pallas_call(
        hand_over,
        out_shape=(
            jax.ShapeDtypeStruct(final.shape, F32),
            jax.ShapeDtypeStruct(coeffs.shape, F32),
        ),
        in_specs=[vmem] * 2,
        out_specs=(pl.BlockSpec(memory_space=pl.ANY), pl.BlockSpec(memory_space=pl.ANY)),
        scratch_shapes=[pltpu.SemaphoreType.DMA((2,))],
        compiler_params=pltpu.CompilerParams(vmem_limit_bytes=4 * 1024 * 1024),
    )(final, coeffs)
    return final.reshape(moments.shape), jnp.transpose(coeffs, (1, 0, 2))


def solution(mesh):
    in_specs = (P(None, "gz", "gy", None), P(), P())
    out_specs = (P(None, "gz", "gy", None), P())
    body = functools.partial(per_device, mesh.shape["gy"], mesh.shape["gz"])
    return jax.shard_map(
        body, mesh=mesh, in_specs=in_specs, out_specs=out_specs, check_vma=False
    )
```

```python
import functools
import math

import jax
import jax.numpy as jnp
import numpy as np
from jax import lax
from jax.experimental import pallas as pl
from jax.experimental.pallas import tpu as pltpu
from jax.sharding import PartitionSpec as P

KMAX = 32
STEPS = 3
RELAX_RATE = 1.6
FORCE_GAIN = 0.5
LANES = 128
MESH = pl.DeviceIdType.MESH
F32 = jnp.float32
BF16 = jnp.bfloat16


def split_np(table):
    high = table.astype(np.float32).astype(jnp.bfloat16)
    low = (table.astype(np.float32) - high.astype(np.float32)).astype(jnp.bfloat16)
    return np.stack([high, low])


def paired(table):
    high, low = split_np(table)
    return np.block([[high, low], [high, np.zeros_like(low)]])


def split(value):
    high = value.astype(BF16)
    return high, (value - high.astype(F32)).astype(BF16)


def dot(lhs, rhs, lhs_dim, rhs_dim):
    return lax.dot_general(
        lhs, rhs, (((lhs_dim,), (rhs_dim,)), ((), ())), preferred_element_type=F32
    )


def dot3(lhs, rhs, lhs_dim, rhs_dim):
    return (
        dot(lhs[0], rhs[0], lhs_dim, rhs_dim)
        + dot(lhs[0], rhs[1], lhs_dim, rhs_dim)
        + dot(lhs[1], rhs[0], lhs_dim, rhs_dim)
    )


def dot_paired(lhs, table):
    both = dot(jnp.concatenate(split(lhs), 1), table, 1, 0)
    return both[:, :LANES] + both[:, LANES:]


def modulo(value, count):
    if count & (count - 1) == 0:
        return value & (count - 1)
    return lax.rem(value, count)


def divide(value, count):
    if count & (count - 1) == 0:
        return lax.shift_right_logical(value, count.bit_length() - 1)
    return lax.div(value, count)


def wave_tables(cells_x):
    rows = cells_x // LANES
    k = np.arange(KMAX)
    alpha = 2 * np.pi * ((np.arange(rows)[:, None] * LANES * k) % cells_x) / cells_x
    phi = 2 * np.pi * ((np.arange(LANES)[:, None] * k) % cells_x) / cells_x
    ca, sa, cp, sp = np.cos(alpha), np.sin(alpha), np.cos(phi), np.sin(phi)
    forward = np.concatenate([ca, sa, -sa, ca], 1)
    forward_fine = np.concatenate([cp, cp, sp, sp], 1)
    inverse = np.concatenate([ca, ca, sa, sa], 1)
    inverse_fine = np.concatenate([cp, sp, cp, sp], 1)
    fine = np.stack([paired(forward_fine), paired(inverse_fine.T)])
    coarse = np.stack([forward, inverse]).astype(np.float32)
    return (jnp.asarray(coarse), jnp.asarray(fine))


def plane_tables(count_gy, count_gz, depth):
    length_y, length_z = count_gy, count_gz * depth
    waves_y, waves_z = min(KMAX, length_y), min(KMAX, length_z)
    device = np.arange(count_gy * count_gz)
    y = np.tile(device // count_gz, depth)
    z = np.concatenate([(device % count_gz) * depth + s for s in range(depth)])
    q = np.arange(waves_y * waves_z)
    phase = (y[:, None] * (q // waves_z) % length_y) / length_y
    phase = phase + (z[:, None] * (q % waves_z) % length_z) / length_z
    cos, sin = np.cos(2 * np.pi * phase), np.sin(2 * np.pi * phase)
    by_source = np.concatenate([cos, sin], 1)
    by_wave = np.concatenate([cos.T, sin.T], 1)
    return (jnp.asarray(split_np(by_source)), jnp.asarray(split_np(by_wave)))


def roll_x(value, shift, lane):
    rows = value.shape[0]
    if shift == 1:
        moved = pltpu.roll(value, 1, 1)
        return jnp.where(lane == 0, pltpu.roll(moved, 1, 0), moved)
    moved = pltpu.roll(value, LANES - 1, 1)
    return jnp.where(lane == LANES - 1, pltpu.roll(moved, rows - 1, 0), moved)


def populations(m, lane):
    rho, jx, jy, jz, pxx, pyy, pzz, pxy, pxz, pyz = m
    trace = 1.5 * (pxx + pyy + pzz)
    out = {(0, 0, 0): (2.5 * rho - trace) * (1.0 / 3.0)}
    base = rho - trace
    j = (jx, jy, jz)
    diag = (4.5 * pxx, 4.5 * pyy, 4.5 * pzz)
    for a in range(3):
        even = (base + diag[a]) * (1.0 / 18.0)
        odd = j[a] * (1.0 / 6.0)
        e = [0, 0, 0]
        e[a] = 1
        out[tuple(e)] = even + odd
        e[a] = -1
        out[tuple(e)] = even - odd
    base = -0.5 * rho - trace
    for a, b, cross in ((0, 1, pxy), (0, 2, pxz), (1, 2, pyz)):
        even = (base + (diag[a] + diag[b])) * (1.0 / 36.0)
        quarter = 0.25 * cross
        plus, minus = even + quarter, even - quarter
        total, diff = (j[a] + j[b]) * (1.0 / 12.0), (j[a] - j[b]) * (1.0 / 12.0)
        for sa, sb, value in (
            (1, 1, plus + total),
            (-1, -1, plus - total),
            (1, -1, minus + diff),
            (-1, 1, minus - diff),
        ):
            e = [0, 0, 0]
            e[a], e[b] = sa, sb
            out[tuple(e)] = value
    return {e: (roll_x(v, e[0], lane) if e[0] else v) for e, v in out.items()}


def local_totals(same, inner, e_in):
    s0, d0 = same[1] + same[-1], same[1] - same[-1]
    s1, d1 = inner[1] + inner[-1], inner[1] - inner[-1]
    layer = inner[0] + s1
    return (same[0] + s0 + layer, d0 + d1, e_in * layer, s0 + s1, layer, e_in * d1)


def totals_of(local, y, z, d, e_in):
    (s_up, x_up, e_up), (s_down, x_down, e_down) = y
    s_z, x_z = z
    up, down = s_up + d[0], s_down + d[1]
    crossing = s_z + (d[0] + d[1])
    within = e_up + e_down
    rho = local[0] + (up + down) + s_z
    jx = local[1] + (x_up + x_down) + x_z
    jy = up - down
    jz = local[2] + e_in * (within - crossing)
    pyy = up + down
    pzz = local[4] + (within + crossing)
    pxy = x_up - x_down
    pxz = local[5] - e_in * x_z
    pyz = e_in * ((e_up - e_down) - (d[0] - d[1]))
    return [rho, jx, jy, jz, None, pyy, pzz, pxy, pxz, pyz]


PAIR_LIST = ((0, 0), (1, 1), (2, 2), (0, 1), (0, 2), (1, 2))


def collide(totals, force, inverse):
    density = totals[0]
    shifted = [(totals[1 + a] + 0.5 * force[a]) * inverse for a in range(3)]
    result = [density] + [totals[1 + a] + force[a] for a in range(3)]
    third = density * (1.0 / 3.0)
    for index, (a, b) in enumerate(PAIR_LIST):
        equilibrium = density * shifted[a] * shifted[b]
        if a == b:
            equilibrium = equilibrium + third
        result.append(
            RELAX_RATE * equilibrium + (1.0 - RELAX_RATE) * totals[4 + index]
        )
    return result


def kernel(
    count_gy, count_gz, gain_scale, normalizer,
    moments_in, wavenumbers_in, gain_in, coarse_in, fine_in, source_in, wave_in,
    final, coeffs,
    moments, wavenumbers, gain, coarse_tables, fine, source_tables, wave_tables_ref,
    load, gathered, filters, send_halo, recv_halo,
    gather_send, gather_recv, first_sems, rest_sems, last_sems,
):
    depth, rows = moments.shape[1:3]
    devices = count_gy * count_gz
    my_y, my_z = lax.axis_index("gy"), lax.axis_index("gz")
    me = my_y * count_gz + my_z
    lane = lax.broadcasted_iota(jnp.int32, (rows, LANES), 1)
    lane1 = lax.broadcasted_iota(jnp.int32, (1, LANES), 1)

    def peer(i):
        if devices & (devices - 1) == 0:
            target = me ^ i
        else:
            target = modulo(me + i, devices)
        return (divide(target, count_gz), modulo(target, count_gz))

    barrier = pltpu.get_barrier_semaphore()

    def greet(i, carry):
        pl.semaphore_signal(barrier, inc=1, device_id=peer(devices - i), device_id_type=MESH)
        return carry

    lax.fori_loop(1, devices, greet, 0)

    loads = [
        pltpu.make_async_copy(src, dst, load.at[i])
        for i, (src, dst) in enumerate((
            (moments_in, moments), (coarse_in, coarse_tables), (fine_in, fine),
            (wavenumbers_in, wavenumbers), (gain_in, gain), (source_in, source_tables),
            (wave_in, wave_tables_ref),
        ))
    ]
    for copy in loads:
        copy.start()

    def y_at(step):
        return modulo(my_y + step + count_gy, count_gy)

    def z_at(step):
        return modulo(my_z + step + count_gz, count_gz)

    first_rows = ((0, 16), (1, 8), (2, 6))

    def rest_rows(step):
        start, count = first_rows[step]
        spans = [(start + count, rows - start - count)]
        return spans + [(0, start)] if start else spans

    early_kinds, all_kinds = 20, 26
    if count_gz == 2:
        early = [(16, 2, 1, 1), (18, 2, -1, 1), (0, 6, 1, 0), (6, 6, -1, 0), (12, 4, 0, 1)]
        late = [(20, 2, 1, 0), (22, 2, -1, 0), (24, 2, 0, 1)]
    else:
        early = [
            (16, 1, 1, 1), (17, 1, 1, -1), (18, 1, -1, 1), (19, 1, -1, -1),
            (0, 6, 1, 0), (6, 6, -1, 0), (12, 2, 0, 1), (14, 2, 0, -1),
        ]
        late = [(20, 2, 1, 0), (22, 2, -1, 0), (24, 1, 0, 1), (25, 1, 0, -1)]

    def send_rows(step, values, base, messages, spans, sems):
        for kind, kinds, dy, dz in messages:
            for start, count in spans:
                for k in range(kind, kind + kinds):
                    send_halo[step, k, start : start + count] = values[k][
                        start - base : start - base + count
                    ]
                part = (step, pl.ds(kind, kinds), pl.ds(start, count))
                pltpu.make_async_remote_copy(
                    src_ref=send_halo.at[part], dst_ref=recv_halo.at[part],
                    send_sem=sems.at[0, step], recv_sem=sems.at[1, step],
                    device_id=(y_at(dy), z_at(dz)), device_id_type=MESH,
                ).start()

    def send_first(step, values, base):
        send_rows(step, values, base, early + late, [first_rows[step]], first_sems)

    def send_rest(step, values):
        send_rows(step, values, 0, early, rest_rows(step), rest_sems)
        send_rows(step, values, 0, late, rest_rows(step), last_sems)

    def wait_rows(step, ref, kinds, count, sem):
        part = ref.at[step, pl.ds(0, kinds), pl.ds(0, count)]
        pltpu.make_async_copy(part, part, sem).wait()

    def wait_first(step, ref, side):
        wait_rows(step, ref, all_kinds, first_rows[step][1], first_sems.at[side, step])

    def wait_rest(step, ref, side):
        wait_rows(step, ref, early_kinds, rows - first_rows[step][1], rest_sems.at[side, step])

    def wait_last(step, ref, side):
        count = rows - first_rows[step][1]
        wait_rows(step, ref, all_kinds - early_kinds, count, last_sems.at[side, step])

    def send_gather(step):
        def send(i, carry):
            pltpu.make_async_remote_copy(
                src_ref=gathered.at[step, me], dst_ref=gathered.at[step, me],
                send_sem=gather_send.at[step], recv_sem=gather_recv.at[step],
                device_id=peer(devices - i), device_id_type=MESH,
            ).start()
            return carry

        if devices <= 32:
            for i in range(1, devices):
                send(i, 0)
        else:
            lax.fori_loop(1, devices, send, 0)

    def wait_for(ref, sem):
        pltpu.make_async_copy(ref, ref, sem).wait()

    waves_y, waves_z = min(KMAX, count_gy), min(KMAX, count_gz * depth)
    modes = wavenumbers.shape[1]

    def wave_onehot():
        q = modulo(wavenumbers[1:2, :], count_gy) * waves_z
        q = q + modulo(wavenumbers[2:3, :], count_gz * depth)
        index = lax.broadcasted_iota(jnp.int32, (waves_y * waves_z, modes), 0)
        return jnp.where(index == q, 1.0, 0.0)

    def x_onehot():
        index = lax.broadcasted_iota(jnp.int32, (KMAX, modes), 0)
        return jnp.where(index == wavenumbers[0:1, :], 1.0, 0.0)

    def build_filters():
        count_q = waves_y * waves_z
        onehot_q = wave_onehot()
        weighted = split(onehot_q * gain[...])
        onehot_x = x_onehot().astype(BF16)
        onehot_x = jnp.concatenate([onehot_x] * 4, 0)
        energy = dot(weighted[0], onehot_x, 1, 1) + dot(weighted[1], onehot_x, 1, 1)
        energy = energy * gain_scale
        index = lax.broadcasted_iota(jnp.int32, (count_q, LANES), 0)
        wave_y, wave_z = divide(index, waves_z), modulo(index, waves_z)
        length_z = count_gz * depth
        phase_y = modulo(wave_y * my_y, count_gy).astype(F32) * (1.0 / count_gy)
        for t in range(depth):
            phase = modulo(wave_z * (my_z * depth + t), length_z).astype(F32)
            angle = (2.0 * math.pi) * (phase_y + phase * (1.0 / length_z))
            ec, es = energy * jnp.cos(angle), energy * jnp.sin(angle)
            for part, stack in enumerate(((ec, es), (es, -ec))):
                pieces = split(jnp.concatenate(stack, 0))
                table = dot3((source_tables[0], source_tables[1]), pieces, 1, 0)
                filters[2 * t + part] = jnp.where(
                    lane1 < LANES // 2, table[:devices], table[devices:]
                )

    def store_coeffs(spectra):
        half = LANES // 2
        sign = jnp.where((lane1 & KMAX) == 0, -1.0, 1.0)
        blocks = []
        for a in range(3):
            top = jnp.concatenate([spectra[a], pltpu.roll(spectra[a], half, 1)], 0)
            swapped = jnp.where((lane1 & KMAX) == 0, pltpu.roll(top, LANES - KMAX, 1), pltpu.roll(top, KMAX, 1))
            blocks.append(jnp.concatenate([top, sign * swapped], 0)[:, :half])
        stacked = jnp.concatenate(blocks, 1)
        transform = dot3((wave_tables_ref[0], wave_tables_ref[1]), split(stacked), 1, 0) * normalizer
        pieces = split(transform)
        onehot_q = wave_onehot().astype(BF16)
        chosen = dot(pieces[0], onehot_q, 0, 0) + dot(pieces[1], onehot_q, 0, 0)
        onehot_x = x_onehot()
        for a in range(3):
            for part in range(2):
                start = (2 * a + part) * KMAX
                picked = jnp.sum(chosen[start : start + KMAX] * onehot_x, axis=0, keepdims=True)
                coeffs[a, part : part + 1, :] = picked

    def partial_waves(speed, start, count):
        stacked = jnp.concatenate([speed[z][a] for z in range(depth) for a in range(3)], 0)
        coarse = dot_paired(stacked, fine[0])
        table = coarse_tables[0, start : start + count]
        return [
            jnp.sum(coarse[r * count : (r + 1) * count] * table, axis=0, keepdims=True)
            for r in range(3 * depth)
        ]

    def project(step, parts):
        folded = [part + pltpu.roll(part, LANES // 2, 1) for part in parts]
        for a in range(3):
            packed = jnp.where(lane1 < LANES // 2, folded[a], folded[3 + a])
            gathered[step, me, :, a * LANES : (a + 1) * LANES] = packed

    def make_force(spectra):
        inverse_coarse = coarse_tables[1]
        swap_sign = jnp.where((lane1 & KMAX) == 0, 1.0, -1.0)
        outer_sign = jnp.where(lane1 < 3 * KMAX, 1.0, -1.0)
        expanded = []
        for z in range(depth):
            for a in range(3):
                first = jnp.sum(spectra[a] * filters[2 * z], axis=0, keepdims=True)
                second = jnp.sum(spectra[a] * filters[2 * z + 1], axis=0, keepdims=True)
                first = first + pltpu.roll(first, LANES // 2, 1)
                second = second + pltpu.roll(second, LANES // 2, 1)
                both = first + swap_sign * pltpu.roll(second, KMAX, 1)
                row = jnp.where(
                    lane1 < LANES // 2, both, outer_sign * pltpu.roll(both, KMAX, 1)
                )
                expanded.append(inverse_coarse * row)
        force = dot_paired(jnp.concatenate(expanded, 0), fine[1])
        return [
            [force[(3 * z + a) * rows : (3 * z + a + 1) * rows] for a in range(3)]
            for z in range(depth)
        ]

    inside = (-1, 1)

    def halo_values(pops):
        values = {}
        for z in range(2):
            e_in, other = inside[z], pops[1 - z]
            for i, sy in enumerate((1, -1)):
                plus, minus = pops[z][1, sy, 0], pops[z][-1, sy, 0]
                both, crossing = plus + minus, other[0, sy, e_in]
                kind = 6 * i + 3 * z
                values[kind] = (pops[z][0, sy, 0] + both) + crossing
                values[kind + 1] = plus - minus
                values[kind + 2] = crossing
                values[20 + 2 * i + z] = both
                values[16 + 2 * i + z] = other[0, sy, -e_in]
            plus, minus = other[1, 0, -e_in], other[-1, 0, -e_in]
            both = plus + minus
            values[12 + 2 * z] = other[0, 0, -e_in] + both
            values[13 + 2 * z] = plus - minus
            values[24 + z] = both
        return values

    def stream(step, local, start, count):
        span = slice(start, start + count)
        totals = []
        for z in range(depth):
            y = [[recv_halo[step, 6 * i + 3 * z + n, span] for n in range(3)] for i in range(2)]
            totals.append(
                totals_of(
                    [value[span] for value in local[z]], y,
                    [recv_halo[step, 12 + 2 * z + n, span] for n in range(2)],
                    [recv_halo[step, 16 + 2 * i + z, span] for i in range(2)], float(inside[z]),
                )
            )
        return totals, [1.0 / totals[z][0] for z in range(depth)]

    def finish(step, local, start, count, totals, force, inverse):
        span = slice(start, start + count)
        out = []
        for z in range(depth):
            up, down, side = [recv_halo[step, 20 + 2 * n + z, span] for n in range(3)]
            totals[z][4] = local[z][3][span] + (up + down) + side
            piece = [value[span] for value in force[z]]
            out.append(collide(totals[z], piece, inverse[z]))
        return out

    def own_totals(pops):
        out = []
        for z in range(2):
            same = {sx: pops[z][sx, 0, 0] for sx in (0, 1, -1)}
            inner = {sx: pops[1 - z][sx, 0, inside[z]] for sx in (0, 1, -1)}
            out.append(local_totals(same, inner, float(inside[z])))
        return out

    def speeds(layers, inverse):
        return [[layers[z][1 + a] * inverse[z] for a in range(3)] for z in range(depth)]

    for copy in loads[:3]:
        copy.wait()
    layers = [[moments[i, z] for i in range(10)] for z in range(depth)]
    speed = speeds(layers, [1.0 / layers[z][0] for z in range(depth)])
    project(0, partial_waves(speed, 0, rows))
    pops = [populations(layers[z], lane) for z in range(depth)]
    values = halo_values(pops)
    pl.semaphore_wait(barrier, devices - 1)
    send_gather(0)
    send_first(0, values, 0)
    send_rest(0, values)
    for copy in loads[3:]:
        copy.wait()
    build_filters()

    for step in range(STEPS):
        last = step == STEPS - 1
        local = own_totals(pops)
        wait_for(gathered.at[step, pl.ds(0, devices - 1)], gather_recv.at[step])
        spectra = [gathered[step, :, 0, a * LANES : (a + 1) * LANES] for a in range(3)]
        force = make_force(spectra)
        if last:
            store_coeffs(spectra)
        wait_first(step, recv_halo, 1)
        if not last:
            start, count = (0, 16) if step == 0 else (1, 8)
            totals, inverse = stream(step, local, start, count)
            ahead = finish(step, local, start, count, totals, force, inverse)
            if step == 0:
                ahead_parts = partial_waves(speeds(ahead, inverse), start, count)
            ahead = [populations(ahead[z], lane[:count]) for z in range(depth)]
            send_first(step + 1, halo_values(ahead), start)
        wait_rest(step, recv_halo, 1)
        totals, inverse = stream(step, local, 0, rows)
        if not last:
            moved = [
                [None] + [totals[z][1 + a] + force[z][a] for a in range(3)] for z in range(depth)
            ]
            speed = speeds(moved, inverse)
            if step == 0:
                speed = [[value[count:] for value in speed[z]] for z in range(depth)]
                parts = partial_waves(speed, count, rows - count)
                parts = [one + two for one, two in zip(ahead_parts, parts)]
            else:
                parts = partial_waves(speed, 0, rows)
            project(step + 1, parts)
            send_gather(step + 1)
        wait_last(step, recv_halo, 1)
        results = finish(step, local, 0, rows, totals, force, inverse)
        if last:
            for z in range(depth):
                for i in range(10):
                    final[i, z] = results[z][i]
        else:
            pops = [populations(results[z], lane) for z in range(depth)]
            send_rest(step + 1, halo_values(pops))

    for step in range(STEPS):
        wait_for(gathered.at[step, pl.ds(0, devices - 1)], gather_send.at[step])
        wait_first(step, send_halo, 0)
        wait_rest(step, send_halo, 0)
        wait_last(step, send_halo, 0)


def hand_over(final_in, coeffs_in, final_out, coeffs_out, sems):
    copies = [
        pltpu.make_async_copy(final_in, final_out, sems.at[0]),
        pltpu.make_async_copy(coeffs_in, coeffs_out, sems.at[1]),
    ]
    for copy in copies:
        copy.start()
    for copy in copies:
        copy.wait()


def per_device(count_gy, count_gz, moments, wavenumbers, mode_gain):
    depth, height, cells_x = moments.shape[1:]
    assert height == 1 and depth == 2 and cells_x % 1024 == 0 and cells_x >= 4096
    rows = cells_x // LANES
    modes = mode_gain.shape[0]
    devices = count_gy * count_gz
    normalizer = 1.0 / math.sqrt(cells_x * height * depth * devices)
    force_scale = FORCE_GAIN / math.sqrt(2 * modes * devices)
    tables = wave_tables(cells_x) + plane_tables(count_gy, count_gz, depth)
    operands = (moments.reshape(10, depth, rows, LANES), wavenumbers, mode_gain.reshape(1, modes)) + tables
    vmem = pl.BlockSpec(memory_space=pltpu.VMEM)
    final, coeffs = pl.pallas_call(
        functools.partial(kernel, count_gy, count_gz, force_scale * normalizer, normalizer),
        out_shape=(
            pltpu.VMEM((10, depth, rows, LANES), F32),
            pltpu.VMEM((3, 2, modes), F32),
        ),
        in_specs=[pl.BlockSpec(memory_space=pl.ANY)] * len(operands),
        out_specs=(vmem, vmem),
        scratch_shapes=[pltpu.VMEM(x.shape, x.dtype) for x in operands] + [
            pltpu.SemaphoreType.DMA((len(operands),)),
            pltpu.VMEM((STEPS, devices, 1, 3 * LANES), F32),
            pltpu.VMEM((2 * depth, devices, LANES), F32),
            pltpu.VMEM((STEPS, 26, rows, LANES), F32),
            pltpu.VMEM((STEPS, 26, rows, LANES), F32),
            pltpu.SemaphoreType.DMA((STEPS,)),
            pltpu.SemaphoreType.DMA((STEPS,)),
            pltpu.SemaphoreType.DMA((2, STEPS)),
            pltpu.SemaphoreType.DMA((2, STEPS)),
            pltpu.SemaphoreType.DMA((2, STEPS)),
        ],
        compiler_params=pltpu.CompilerParams(
            collective_id=0, has_side_effects=True, vmem_limit_bytes=60 * 1024 * 1024
        ),
    )(*operands)
    final, coeffs = pl.pallas_call(
        hand_over,
        out_shape=(
            jax.ShapeDtypeStruct(final.shape, F32),
            jax.ShapeDtypeStruct(coeffs.shape, F32),
        ),
        in_specs=[vmem] * 2,
        out_specs=(pl.BlockSpec(memory_space=pl.ANY), pl.BlockSpec(memory_space=pl.ANY)),
        scratch_shapes=[pltpu.SemaphoreType.DMA((2,))],
        compiler_params=pltpu.CompilerParams(vmem_limit_bytes=4 * 1024 * 1024),
    )(final, coeffs)
    return final.reshape(moments.shape), jnp.transpose(coeffs, (1, 0, 2))


def solution(mesh):
    in_specs = (P(None, "gz", "gy", None), P(), P())
    out_specs = (P(None, "gz", "gy", None), P())
    body = functools.partial(per_device, mesh.shape["gy"], mesh.shape["gz"])
    return jax.shard_map(
        body, mesh=mesh, in_specs=in_specs, out_specs=out_specs, check_vma=False
    )
```

```python
import functools
import math

import jax
import jax.numpy as jnp
import numpy as np
from jax import lax
from jax.experimental import pallas as pl
from jax.experimental.pallas import tpu as pltpu
from jax.sharding import PartitionSpec as P

KMAX = 32
STEPS = 3
RELAX_RATE = 1.6
FORCE_GAIN = 0.5
LANES = 128
MESH = pl.DeviceIdType.MESH
F32 = jnp.float32
BF16 = jnp.bfloat16


def split_np(table):
    high = table.astype(np.float32).astype(jnp.bfloat16)
    low = (table.astype(np.float32) - high.astype(np.float32)).astype(jnp.bfloat16)
    return np.stack([high, low])


def paired(table):
    high, low = split_np(table)
    return np.block([[high, low], [high, np.zeros_like(low)]])


def split(value):
    high = value.astype(BF16)
    return high, (value - high.astype(F32)).astype(BF16)


def dot(lhs, rhs, lhs_dim, rhs_dim):
    return lax.dot_general(
        lhs, rhs, (((lhs_dim,), (rhs_dim,)), ((), ())), preferred_element_type=F32
    )


def dot3(lhs, rhs, lhs_dim, rhs_dim):
    return (
        dot(lhs[0], rhs[0], lhs_dim, rhs_dim)
        + dot(lhs[0], rhs[1], lhs_dim, rhs_dim)
        + dot(lhs[1], rhs[0], lhs_dim, rhs_dim)
    )


def dot_paired(lhs, table):
    both = dot(jnp.concatenate(split(lhs), 1), table, 1, 0)
    return both[:, :LANES] + both[:, LANES:]


def modulo(value, count):
    if count & (count - 1) == 0:
        return value & (count - 1)
    return lax.rem(value, count)


def divide(value, count):
    if count & (count - 1) == 0:
        return lax.shift_right_logical(value, count.bit_length() - 1)
    return lax.div(value, count)


def wave_tables(cells_x):
    rows = cells_x // LANES
    k = np.arange(KMAX)
    alpha = 2 * np.pi * ((np.arange(rows)[:, None] * LANES * k) % cells_x) / cells_x
    phi = 2 * np.pi * ((np.arange(LANES)[:, None] * k) % cells_x) / cells_x
    ca, sa, cp, sp = np.cos(alpha), np.sin(alpha), np.cos(phi), np.sin(phi)
    forward = np.concatenate([ca, sa, -sa, ca], 1)
    forward_fine = np.concatenate([cp, cp, sp, sp], 1)
    inverse = np.concatenate([ca, ca, sa, sa], 1)
    inverse_fine = np.concatenate([cp, sp, cp, sp], 1)
    fine = np.stack([paired(forward_fine), paired(inverse_fine.T)])
    coarse = np.stack([forward, inverse]).astype(np.float32)
    return (jnp.asarray(coarse), jnp.asarray(fine))


def plane_tables(count_gy, count_gz, depth):
    length_y, length_z = count_gy, count_gz * depth
    waves_y, waves_z = min(KMAX, length_y), min(KMAX, length_z)
    device = np.arange(count_gy * count_gz)
    y = np.tile(device // count_gz, depth)
    z = np.concatenate([(device % count_gz) * depth + s for s in range(depth)])
    q = np.arange(waves_y * waves_z)
    phase = (y[:, None] * (q // waves_z) % length_y) / length_y
    phase = phase + (z[:, None] * (q % waves_z) % length_z) / length_z
    cos, sin = np.cos(2 * np.pi * phase), np.sin(2 * np.pi * phase)
    by_source = np.concatenate([cos, sin], 1)
    by_wave = np.concatenate([cos.T, sin.T], 1)
    return (jnp.asarray(split_np(by_source)), jnp.asarray(split_np(by_wave)))


def roll_x(value, shift, lane):
    rows = value.shape[0]
    if shift == 1:
        moved = pltpu.roll(value, 1, 1)
        return jnp.where(lane == 0, pltpu.roll(moved, 1, 0), moved)
    moved = pltpu.roll(value, LANES - 1, 1)
    return jnp.where(lane == LANES - 1, pltpu.roll(moved, rows - 1, 0), moved)


def populations(m, lane):
    rho, jx, jy, jz, pxx, pyy, pzz, pxy, pxz, pyz = m
    trace = 1.5 * (pxx + pyy + pzz)
    out = {(0, 0, 0): (2.5 * rho - trace) * (1.0 / 3.0)}
    base = rho - trace
    j = (jx, jy, jz)
    diag = (4.5 * pxx, 4.5 * pyy, 4.5 * pzz)
    for a in range(3):
        even = (base + diag[a]) * (1.0 / 18.0)
        odd = j[a] * (1.0 / 6.0)
        e = [0, 0, 0]
        e[a] = 1
        out[tuple(e)] = even + odd
        e[a] = -1
        out[tuple(e)] = even - odd
    base = -0.5 * rho - trace
    for a, b, cross in ((0, 1, pxy), (0, 2, pxz), (1, 2, pyz)):
        even = (base + (diag[a] + diag[b])) * (1.0 / 36.0)
        quarter = 0.25 * cross
        plus, minus = even + quarter, even - quarter
        total, diff = (j[a] + j[b]) * (1.0 / 12.0), (j[a] - j[b]) * (1.0 / 12.0)
        for sa, sb, value in (
            (1, 1, plus + total),
            (-1, -1, plus - total),
            (1, -1, minus + diff),
            (-1, 1, minus - diff),
        ):
            e = [0, 0, 0]
            e[a], e[b] = sa, sb
            out[tuple(e)] = value
    return {e: (roll_x(v, e[0], lane) if e[0] else v) for e, v in out.items()}


def local_totals(same, inner, e_in):
    s0, d0 = same[1] + same[-1], same[1] - same[-1]
    s1, d1 = inner[1] + inner[-1], inner[1] - inner[-1]
    layer = inner[0] + s1
    return (same[0] + s0 + layer, d0 + d1, e_in * layer, s0 + s1, layer, e_in * d1)


def totals_of(local, y, z, d, e_in):
    (s_up, x_up, e_up), (s_down, x_down, e_down) = y
    s_z, x_z = z
    up, down = s_up + d[0], s_down + d[1]
    crossing = s_z + (d[0] + d[1])
    within = e_up + e_down
    rho = local[0] + (up + down) + s_z
    jx = local[1] + (x_up + x_down) + x_z
    jy = up - down
    jz = local[2] + e_in * (within - crossing)
    pyy = up + down
    pzz = local[4] + (within + crossing)
    pxy = x_up - x_down
    pxz = local[5] - e_in * x_z
    pyz = e_in * ((e_up - e_down) - (d[0] - d[1]))
    return [rho, jx, jy, jz, None, pyy, pzz, pxy, pxz, pyz]


PAIR_LIST = ((0, 0), (1, 1), (2, 2), (0, 1), (0, 2), (1, 2))


def collide(totals, force, inverse):
    density = totals[0]
    shifted = [(totals[1 + a] + 0.5 * force[a]) * inverse for a in range(3)]
    result = [density] + [totals[1 + a] + force[a] for a in range(3)]
    third = density * (1.0 / 3.0)
    for index, (a, b) in enumerate(PAIR_LIST):
        equilibrium = density * shifted[a] * shifted[b]
        if a == b:
            equilibrium = equilibrium + third
        result.append(
            RELAX_RATE * equilibrium + (1.0 - RELAX_RATE) * totals[4 + index]
        )
    return result


def kernel(
    count_gy, count_gz, gain_scale, normalizer,
    moments_in, wavenumbers_in, gain_in, coarse_in, fine_in, source_in, wave_in,
    final, coeffs,
    moments, wavenumbers, gain, coarse_tables, fine, source_tables, wave_tables_ref,
    load, gathered, filters, send_halo, recv_halo,
    gather_send, gather_recv, first_sems, rest_sems, last_sems,
):
    depth, rows = moments.shape[1:3]
    devices = count_gy * count_gz
    my_y, my_z = lax.axis_index("gy"), lax.axis_index("gz")
    me = my_y * count_gz + my_z
    lane = lax.broadcasted_iota(jnp.int32, (rows, LANES), 1)
    lane1 = lax.broadcasted_iota(jnp.int32, (1, LANES), 1)

    def peer(i):
        if devices & (devices - 1) == 0:
            target = me ^ i
        else:
            target = modulo(me + i, devices)
        return (divide(target, count_gz), modulo(target, count_gz))

    barrier = pltpu.get_barrier_semaphore()

    def greet(i, carry):
        pl.semaphore_signal(barrier, inc=1, device_id=peer(devices - i), device_id_type=MESH)
        return carry

    lax.fori_loop(1, devices, greet, 0)

    loads = [
        pltpu.make_async_copy(src, dst, load.at[i])
        for i, (src, dst) in enumerate((
            (moments_in, moments), (coarse_in, coarse_tables), (fine_in, fine),
            (wavenumbers_in, wavenumbers), (gain_in, gain), (source_in, source_tables),
            (wave_in, wave_tables_ref),
        ))
    ]
    for copy in loads:
        copy.start()

    def y_at(step):
        return modulo(my_y + step + count_gy, count_gy)

    def z_at(step):
        return modulo(my_z + step + count_gz, count_gz)

    first_rows = ((0, 16), (1, 11), (2, 6))

    def rest_rows(step):
        start, count = first_rows[step]
        spans = [(start + count, rows - start - count)]
        return spans + [(0, start)] if start else spans

    early_kinds, all_kinds = 20, 26
    if count_gz == 2:
        whole = [(22, 2, 1, 1), (24, 2, -1, 1), (0, 8, 1, 0), (8, 8, -1, 0), (16, 6, 0, 1)]
        early = [(22, 2, 1, 1), (24, 2, -1, 1), (0, 6, 1, 0), (8, 6, -1, 0), (16, 4, 0, 1)]
        late = [(6, 2, 1, 0), (14, 2, -1, 0), (20, 2, 0, 1)]
    else:
        early = [
            (22, 1, 1, 1), (23, 1, 1, -1), (24, 1, -1, 1), (25, 1, -1, -1),
            (0, 6, 1, 0), (8, 6, -1, 0), (16, 2, 0, 1), (18, 2, 0, -1),
        ]
        late = [(6, 2, 1, 0), (14, 2, -1, 0), (20, 1, 0, 1), (21, 1, 0, -1)]
        whole = early + late

    def send_rows(step, values, base, messages, spans, sems):
        for kind, kinds, dy, dz in messages:
            for start, count in spans:
                for k in range(kind, kind + kinds) if values else ():
                    send_halo[step, k, start : start + count] = values[k][
                        start - base : start - base + count
                    ]
                part = (step, pl.ds(kind, kinds), pl.ds(start, count))
                pltpu.make_async_remote_copy(
                    src_ref=send_halo.at[part], dst_ref=recv_halo.at[part],
                    send_sem=sems.at[0, step], recv_sem=sems.at[1, step],
                    device_id=(y_at(dy), z_at(dz)), device_id_type=MESH,
                ).start()

    def send_first(step, values, base):
        send_rows(step, values, base, whole, [first_rows[step]], first_sems)

    def send_rest(step, values):
        send_rows(step, values, 0, early, rest_rows(step), rest_sems)
        send_rows(step, values, 0, late, rest_rows(step), last_sems)

    def wait_rows(step, ref, kinds, count, sem):
        part = ref.at[step, pl.ds(0, kinds), pl.ds(0, count)]
        pltpu.make_async_copy(part, part, sem).wait()

    def wait_first(step, ref, side):
        wait_rows(step, ref, all_kinds, first_rows[step][1], first_sems.at[side, step])

    def wait_rest(step, ref, side):
        wait_rows(step, ref, early_kinds, rows - first_rows[step][1], rest_sems.at[side, step])

    def wait_last(step, ref, side):
        count = rows - first_rows[step][1]
        wait_rows(step, ref, all_kinds - early_kinds, count, last_sems.at[side, step])

    def send_gather(step):
        def send(i, carry):
            pltpu.make_async_remote_copy(
                src_ref=gathered.at[step, me], dst_ref=gathered.at[step, me],
                send_sem=gather_send.at[step], recv_sem=gather_recv.at[step],
                device_id=peer(devices - i), device_id_type=MESH,
            ).start()
            return carry

        if devices <= 32:
            for i in range(1, devices):
                send(i, 0)
        else:
            lax.fori_loop(1, devices, send, 0)

    def wait_for(ref, sem):
        pltpu.make_async_copy(ref, ref, sem).wait()

    waves_y, waves_z = min(KMAX, count_gy), min(KMAX, count_gz * depth)
    modes = wavenumbers.shape[1]

    def wave_onehot():
        q = modulo(wavenumbers[1:2, :], count_gy) * waves_z
        q = q + modulo(wavenumbers[2:3, :], count_gz * depth)
        index = lax.broadcasted_iota(jnp.int32, (waves_y * waves_z, modes), 0)
        return jnp.where(index == q, 1.0, 0.0)

    def x_onehot():
        index = lax.broadcasted_iota(jnp.int32, (KMAX, modes), 0)
        return jnp.where(index == wavenumbers[0:1, :], 1.0, 0.0)

    def build_filters():
        count_q = waves_y * waves_z
        onehot_q = wave_onehot()
        weighted = split(onehot_q * gain[...])
        onehot_x = x_onehot().astype(BF16)
        onehot_x = jnp.concatenate([onehot_x] * 4, 0)
        energy = dot(weighted[0], onehot_x, 1, 1) + dot(weighted[1], onehot_x, 1, 1)
        energy = energy * gain_scale
        index = lax.broadcasted_iota(jnp.int32, (count_q, LANES), 0)
        wave_y, wave_z = divide(index, waves_z), modulo(index, waves_z)
        length_z = count_gz * depth
        phase_y = modulo(wave_y * my_y, count_gy).astype(F32) * (1.0 / count_gy)
        for t in range(depth):
            phase = modulo(wave_z * (my_z * depth + t), length_z).astype(F32)
            angle = (2.0 * math.pi) * (phase_y + phase * (1.0 / length_z))
            ec, es = energy * jnp.cos(angle), energy * jnp.sin(angle)
            for part, stack in enumerate(((ec, es), (es, -ec))):
                pieces = split(jnp.concatenate(stack, 0))
                table = dot3((source_tables[0], source_tables[1]), pieces, 1, 0)
                filters[2 * t + part] = jnp.where(
                    lane1 < LANES // 2, table[:devices], table[devices:]
                )

    def store_coeffs(spectra):
        half = LANES // 2
        sign = jnp.where((lane1 & KMAX) == 0, -1.0, 1.0)
        blocks = []
        for a in range(3):
            top = jnp.concatenate([spectra[a], pltpu.roll(spectra[a], half, 1)], 0)
            swapped = jnp.where((lane1 & KMAX) == 0, pltpu.roll(top, LANES - KMAX, 1), pltpu.roll(top, KMAX, 1))
            blocks.append(jnp.concatenate([top, sign * swapped], 0)[:, :half])
        stacked = jnp.concatenate(blocks, 1)
        transform = dot3((wave_tables_ref[0], wave_tables_ref[1]), split(stacked), 1, 0) * normalizer
        pieces = split(transform)
        onehot_q = wave_onehot().astype(BF16)
        chosen = dot(pieces[0], onehot_q, 0, 0) + dot(pieces[1], onehot_q, 0, 0)
        onehot_x = x_onehot()
        for a in range(3):
            for part in range(2):
                start = (2 * a + part) * KMAX
                picked = jnp.sum(chosen[start : start + KMAX] * onehot_x, axis=0, keepdims=True)
                coeffs[a, part : part + 1, :] = picked

    def partial_waves(speed, start, count):
        stacked = jnp.concatenate([speed[z][a] for z in range(depth) for a in range(3)], 0)
        coarse = dot_paired(stacked, fine[0])
        table = coarse_tables[0, start : start + count]
        return [
            jnp.sum(coarse[r * count : (r + 1) * count] * table, axis=0, keepdims=True)
            for r in range(3 * depth)
        ]

    def project(step, parts):
        folded = [part + pltpu.roll(part, LANES // 2, 1) for part in parts]
        for a in range(3):
            packed = jnp.where(lane1 < LANES // 2, folded[a], folded[3 + a])
            gathered[step, me, :, a * LANES : (a + 1) * LANES] = packed

    def make_force(spectra):
        inverse_coarse = coarse_tables[1]
        swap_sign = jnp.where((lane1 & KMAX) == 0, 1.0, -1.0)
        outer_sign = jnp.where(lane1 < 3 * KMAX, 1.0, -1.0)
        expanded = []
        for z in range(depth):
            for a in range(3):
                first = jnp.sum(spectra[a] * filters[2 * z], axis=0, keepdims=True)
                second = jnp.sum(spectra[a] * filters[2 * z + 1], axis=0, keepdims=True)
                first = first + pltpu.roll(first, LANES // 2, 1)
                second = second + pltpu.roll(second, LANES // 2, 1)
                both = first + swap_sign * pltpu.roll(second, KMAX, 1)
                row = jnp.where(
                    lane1 < LANES // 2, both, outer_sign * pltpu.roll(both, KMAX, 1)
                )
                expanded.append(inverse_coarse * row)
        force = dot_paired(jnp.concatenate(expanded, 0), fine[1])
        return [
            [force[(3 * z + a) * rows : (3 * z + a + 1) * rows] for a in range(3)]
            for z in range(depth)
        ]

    inside = (-1, 1)

    def halo_values(pops):
        values = {}
        for z in range(2):
            e_in, other = inside[z], pops[1 - z]
            for i, sy in enumerate((1, -1)):
                plus, minus = pops[z][1, sy, 0], pops[z][-1, sy, 0]
                both, crossing = plus + minus, other[0, sy, e_in]
                kind = 8 * i + 3 * z
                values[kind] = (pops[z][0, sy, 0] + both) + crossing
                values[kind + 1] = plus - minus
                values[kind + 2] = crossing
                values[8 * i + 6 + z] = both
                values[22 + 2 * i + z] = other[0, sy, -e_in]
            plus, minus = other[1, 0, -e_in], other[-1, 0, -e_in]
            both = plus + minus
            values[16 + 2 * z] = other[0, 0, -e_in] + both
            values[17 + 2 * z] = plus - minus
            values[20 + z] = both
        return values

    def stream(step, local, start, count):
        span = slice(start, start + count)
        totals = []
        for z in range(depth):
            y = [[recv_halo[step, 8 * i + 3 * z + n, span] for n in range(3)] for i in range(2)]
            totals.append(
                totals_of(
                    [value[span] for value in local[z]], y,
                    [recv_halo[step, 16 + 2 * z + n, span] for n in range(2)],
                    [recv_halo[step, 22 + 2 * i + z, span] for i in range(2)], float(inside[z]),
                )
            )
        return totals, [1.0 / totals[z][0] for z in range(depth)]

    def finish(step, local, start, count, totals, force, inverse):
        span = slice(start, start + count)
        out = []
        for z in range(depth):
            up, down, side = [recv_halo[step, k + z, span] for k in (6, 14, 20)]
            totals[z][4] = local[z][3][span] + (up + down) + side
            piece = [value[span] for value in force[z]]
            out.append(collide(totals[z], piece, inverse[z]))
        return out

    def own_totals(pops):
        out = []
        for z in range(2):
            same = {sx: pops[z][sx, 0, 0] for sx in (0, 1, -1)}
            inner = {sx: pops[1 - z][sx, 0, inside[z]] for sx in (0, 1, -1)}
            out.append(local_totals(same, inner, float(inside[z])))
        return out

    def speeds(layers, inverse):
        return [[layers[z][1 + a] * inverse[z] for a in range(3)] for z in range(depth)]

    for copy in loads[:3]:
        copy.wait()
    layers = [[moments[i, z] for i in range(10)] for z in range(depth)]
    speed = speeds(layers, [1.0 / layers[z][0] for z in range(depth)])
    project(0, partial_waves(speed, 0, rows))
    pops = [populations(layers[z], lane) for z in range(depth)]
    for k, value in halo_values(pops).items():
        send_halo[0, k] = value
    pl.semaphore_wait(barrier, devices - 1)
    send_gather(0)
    send_first(0, None, 0)
    send_rest(0, None)
    for copy in loads[3:]:
        copy.wait()
    build_filters()

    def wait_sent(step):
        wait_for(gathered.at[step, pl.ds(0, devices - 1)], gather_send.at[step])
        wait_first(step, send_halo, 0)
        wait_rest(step, send_halo, 0)
        wait_last(step, send_halo, 0)

    for step in range(STEPS):
        last = step == STEPS - 1
        local = own_totals(pops)
        wait_for(gathered.at[step, pl.ds(0, devices - 1)], gather_recv.at[step])
        spectra = [gathered[step, :, 0, a * LANES : (a + 1) * LANES] for a in range(3)]
        force = make_force(spectra)
        if last:
            store_coeffs(spectra)
            for done in range(STEPS):
                wait_sent(done)
        wait_first(step, recv_halo, 1)
        if not last:
            start, count = (0, 16) if step == 0 else (1, 8)
            totals, inverse = stream(step, local, start, count)
            ahead = finish(step, local, start, count, totals, force, inverse)
            if step == 0:
                ahead_parts = partial_waves(speeds(ahead, inverse), start, count)
            ahead = [populations(ahead[z], lane[:count]) for z in range(depth)]
            send_first(step + 1, halo_values(ahead), start)
        wait_rest(step, recv_halo, 1)
        totals, inverse = stream(step, local, 0, rows)
        if not last:
            moved = [
                [None] + [totals[z][1 + a] + force[z][a] for a in range(3)] for z in range(depth)
            ]
            speed = speeds(moved, inverse)
            if step == 0:
                speed = [[value[count:] for value in speed[z]] for z in range(depth)]
                parts = partial_waves(speed, count, rows - count)
                parts = [one + two for one, two in zip(ahead_parts, parts)]
            else:
                parts = partial_waves(speed, 0, rows)
            project(step + 1, parts)
            send_gather(step + 1)
        wait_last(step, recv_halo, 1)
        results = finish(step, local, 0, rows, totals, force, inverse)
        if last:
            for z in range(depth):
                for i in range(10):
                    final[i, z] = results[z][i]
        else:
            pops = [populations(results[z], lane) for z in range(depth)]
            send_rest(step + 1, halo_values(pops))


def hand_over(final_in, coeffs_in, final_out, coeffs_out, sems):
    copies = [
        pltpu.make_async_copy(final_in, final_out, sems.at[0]),
        pltpu.make_async_copy(coeffs_in, coeffs_out, sems.at[1]),
    ]
    for copy in copies:
        copy.start()
    for copy in copies:
        copy.wait()


def per_device(count_gy, count_gz, moments, wavenumbers, mode_gain):
    depth, height, cells_x = moments.shape[1:]
    assert height == 1 and depth == 2 and cells_x % 1024 == 0 and cells_x >= 4096
    rows = cells_x // LANES
    modes = mode_gain.shape[0]
    devices = count_gy * count_gz
    normalizer = 1.0 / math.sqrt(cells_x * height * depth * devices)
    force_scale = FORCE_GAIN / math.sqrt(2 * modes * devices)
    tables = wave_tables(cells_x) + plane_tables(count_gy, count_gz, depth)
    operands = (moments.reshape(10, depth, rows, LANES), wavenumbers, mode_gain.reshape(1, modes)) + tables
    vmem = pl.BlockSpec(memory_space=pltpu.VMEM)
    final, coeffs = pl.pallas_call(
        functools.partial(kernel, count_gy, count_gz, force_scale * normalizer, normalizer),
        out_shape=(
            pltpu.VMEM((10, depth, rows, LANES), F32),
            pltpu.VMEM((3, 2, modes), F32),
        ),
        in_specs=[pl.BlockSpec(memory_space=pl.ANY)] * len(operands),
        out_specs=(vmem, vmem),
        scratch_shapes=[pltpu.VMEM(x.shape, x.dtype) for x in operands] + [
            pltpu.SemaphoreType.DMA((len(operands),)),
            pltpu.VMEM((STEPS, devices, 1, 3 * LANES), F32),
            pltpu.VMEM((2 * depth, devices, LANES), F32),
            pltpu.VMEM((STEPS, 26, rows, LANES), F32),
            pltpu.VMEM((STEPS, 26, rows, LANES), F32),
            pltpu.SemaphoreType.DMA((STEPS,)),
            pltpu.SemaphoreType.DMA((STEPS,)),
            pltpu.SemaphoreType.DMA((2, STEPS)),
            pltpu.SemaphoreType.DMA((2, STEPS)),
            pltpu.SemaphoreType.DMA((2, STEPS)),
        ],
        compiler_params=pltpu.CompilerParams(
            collective_id=0, has_side_effects=True, vmem_limit_bytes=60 * 1024 * 1024
        ),
    )(*operands)
    final, coeffs = pl.pallas_call(
        hand_over,
        out_shape=(
            jax.ShapeDtypeStruct(final.shape, F32),
            jax.ShapeDtypeStruct(coeffs.shape, F32),
        ),
        in_specs=[vmem] * 2,
        out_specs=(pl.BlockSpec(memory_space=pl.ANY), pl.BlockSpec(memory_space=pl.ANY)),
        scratch_shapes=[pltpu.SemaphoreType.DMA((2,))],
        compiler_params=pltpu.CompilerParams(vmem_limit_bytes=4 * 1024 * 1024),
    )(final, coeffs)
    return final.reshape(moments.shape), jnp.transpose(coeffs, (1, 0, 2))


def solution(mesh):
    in_specs = (P(None, "gz", "gy", None), P(), P())
    out_specs = (P(None, "gz", "gy", None), P())
    body = functools.partial(per_device, mesh.shape["gy"], mesh.shape["gz"])
    return jax.shard_map(
        body, mesh=mesh, in_specs=in_specs, out_specs=out_specs, check_vma=False
    )
```

```python
import functools
import math

import jax
import jax.numpy as jnp
import numpy as np
from jax import lax
from jax.experimental import pallas as pl
from jax.experimental.pallas import tpu as pltpu
from jax.sharding import PartitionSpec as P

KMAX = 32
STEPS = 3
RELAX_RATE = 1.6
FORCE_GAIN = 0.5
LANES = 128
MESH = pl.DeviceIdType.MESH
F32 = jnp.float32
BF16 = jnp.bfloat16


def split_np(table):
    high = table.astype(np.float32).astype(jnp.bfloat16)
    low = (table.astype(np.float32) - high.astype(np.float32)).astype(jnp.bfloat16)
    return np.stack([high, low])


def paired(table):
    high, low = split_np(table)
    return np.block([[high, low], [high, np.zeros_like(low)]])


def split(value):
    high = value.astype(BF16)
    return high, (value - high.astype(F32)).astype(BF16)


def dot(lhs, rhs, lhs_dim, rhs_dim):
    return lax.dot_general(
        lhs, rhs, (((lhs_dim,), (rhs_dim,)), ((), ())), preferred_element_type=F32
    )


def dot3(lhs, rhs, lhs_dim, rhs_dim):
    return (
        dot(lhs[0], rhs[0], lhs_dim, rhs_dim)
        + dot(lhs[0], rhs[1], lhs_dim, rhs_dim)
        + dot(lhs[1], rhs[0], lhs_dim, rhs_dim)
    )


def dot_paired(lhs, table):
    both = dot(jnp.concatenate(split(lhs), 1), table, 1, 0)
    return both[:, :LANES] + both[:, LANES:]


def modulo(value, count):
    if count & (count - 1) == 0:
        return value & (count - 1)
    return lax.rem(value, count)


def divide(value, count):
    if count & (count - 1) == 0:
        return lax.shift_right_logical(value, count.bit_length() - 1)
    return lax.div(value, count)


def wave_tables(cells_x):
    rows = cells_x // LANES
    k = np.arange(KMAX)
    alpha = 2 * np.pi * ((np.arange(rows)[:, None] * LANES * k) % cells_x) / cells_x
    phi = 2 * np.pi * ((np.arange(LANES)[:, None] * k) % cells_x) / cells_x
    ca, sa, cp, sp = np.cos(alpha), np.sin(alpha), np.cos(phi), np.sin(phi)
    forward = np.concatenate([ca, sa, -sa, ca], 1)
    forward_fine = np.concatenate([cp, cp, sp, sp], 1)
    inverse = np.concatenate([ca, ca, sa, sa], 1)
    inverse_fine = np.concatenate([cp, sp, cp, sp], 1)
    fine = np.stack([paired(forward_fine), paired(inverse_fine.T)])
    coarse = np.stack([forward, inverse]).astype(np.float32)
    return (jnp.asarray(coarse), jnp.asarray(fine))


def plane_tables(count_gy, count_gz, depth):
    length_y, length_z = count_gy, count_gz * depth
    waves_y, waves_z = min(KMAX, length_y), min(KMAX, length_z)
    device = np.arange(count_gy * count_gz)
    y = np.tile(device // count_gz, depth)
    z = np.concatenate([(device % count_gz) * depth + s for s in range(depth)])
    q = np.arange(waves_y * waves_z)
    phase = (y[:, None] * (q // waves_z) % length_y) / length_y
    phase = phase + (z[:, None] * (q % waves_z) % length_z) / length_z
    cos, sin = np.cos(2 * np.pi * phase), np.sin(2 * np.pi * phase)
    by_source = np.concatenate([cos, sin], 1)
    by_wave = np.concatenate([cos.T, sin.T], 1)
    return (jnp.asarray(split_np(by_source)), jnp.asarray(split_np(by_wave)))


def roll_x(value, shift, lane):
    rows = value.shape[0]
    if shift == 1:
        moved = pltpu.roll(value, 1, 1)
        return jnp.where(lane == 0, pltpu.roll(moved, 1, 0), moved)
    moved = pltpu.roll(value, LANES - 1, 1)
    return jnp.where(lane == LANES - 1, pltpu.roll(moved, rows - 1, 0), moved)


def populations(m, lane):
    rho, jx, jy, jz, pxx, pyy, pzz, pxy, pxz, pyz = m
    trace = 1.5 * (pxx + pyy + pzz)
    out = {(0, 0, 0): (2.5 * rho - trace) * (1.0 / 3.0)}
    base = rho - trace
    j = (jx, jy, jz)
    diag = (4.5 * pxx, 4.5 * pyy, 4.5 * pzz)
    for a in range(3):
        even = (base + diag[a]) * (1.0 / 18.0)
        odd = j[a] * (1.0 / 6.0)
        e = [0, 0, 0]
        e[a] = 1
        out[tuple(e)] = even + odd
        e[a] = -1
        out[tuple(e)] = even - odd
    base = -0.5 * rho - trace
    for a, b, cross in ((0, 1, pxy), (0, 2, pxz), (1, 2, pyz)):
        even = (base + (diag[a] + diag[b])) * (1.0 / 36.0)
        quarter = 0.25 * cross
        plus, minus = even + quarter, even - quarter
        total, diff = (j[a] + j[b]) * (1.0 / 12.0), (j[a] - j[b]) * (1.0 / 12.0)
        for sa, sb, value in (
            (1, 1, plus + total),
            (-1, -1, plus - total),
            (1, -1, minus + diff),
            (-1, 1, minus - diff),
        ):
            e = [0, 0, 0]
            e[a], e[b] = sa, sb
            out[tuple(e)] = value
    return {e: (roll_x(v, e[0], lane) if e[0] else v) for e, v in out.items()}


def local_totals(same, inner, e_in):
    s0, d0 = same[1] + same[-1], same[1] - same[-1]
    s1, d1 = inner[1] + inner[-1], inner[1] - inner[-1]
    layer = inner[0] + s1
    return (same[0] + s0 + layer, d0 + d1, e_in * layer, s0 + s1, layer, e_in * d1)


def totals_of(local, y, z, d, e_in):
    (s_up, x_up, e_up), (s_down, x_down, e_down) = y
    s_z, x_z = z
    up, down = s_up + d[0], s_down + d[1]
    crossing = s_z + (d[0] + d[1])
    within = e_up + e_down
    rho = local[0] + (up + down) + s_z
    jx = local[1] + (x_up + x_down) + x_z
    jy = up - down
    jz = local[2] + e_in * (within - crossing)
    pyy = up + down
    pzz = local[4] + (within + crossing)
    pxy = x_up - x_down
    pxz = local[5] - e_in * x_z
    pyz = e_in * ((e_up - e_down) - (d[0] - d[1]))
    return [rho, jx, jy, jz, None, pyy, pzz, pxy, pxz, pyz]


PAIR_LIST = ((0, 0), (1, 1), (2, 2), (0, 1), (0, 2), (1, 2))


def collide(totals, force, inverse):
    density = totals[0]
    shifted = [(totals[1 + a] + 0.5 * force[a]) * inverse for a in range(3)]
    result = [density] + [totals[1 + a] + force[a] for a in range(3)]
    third = density * (1.0 / 3.0)
    for index, (a, b) in enumerate(PAIR_LIST):
        equilibrium = density * shifted[a] * shifted[b]
        if a == b:
            equilibrium = equilibrium + third
        result.append(
            RELAX_RATE * equilibrium + (1.0 - RELAX_RATE) * totals[4 + index]
        )
    return result


def kernel(
    count_gy, count_gz, gain_scale, normalizer,
    moments_in, wavenumbers_in, gain_in, coarse_in, fine_in, source_in, wave_in,
    final, coeffs,
    moments, wavenumbers, gain, coarse_tables, fine, source_tables, wave_tables_ref,
    load, gathered, filters, send_halo, recv_halo,
    gather_send, gather_recv, first_sems, rest_sems, last_sems,
):
    depth, rows = moments.shape[1:3]
    devices = count_gy * count_gz
    my_y, my_z = lax.axis_index("gy"), lax.axis_index("gz")
    me = my_y * count_gz + my_z
    lane = lax.broadcasted_iota(jnp.int32, (rows, LANES), 1)
    lane1 = lax.broadcasted_iota(jnp.int32, (1, LANES), 1)

    def peer(i):
        if devices & (devices - 1) == 0:
            target = me ^ i
        else:
            target = modulo(me + i, devices)
        return (divide(target, count_gz), modulo(target, count_gz))

    barrier = pltpu.get_barrier_semaphore()

    def greet(i, carry):
        pl.semaphore_signal(barrier, inc=1, device_id=peer(devices - i), device_id_type=MESH)
        return carry

    lax.fori_loop(1, devices, greet, 0)

    loads = [
        pltpu.make_async_copy(src, dst, load.at[i])
        for i, (src, dst) in enumerate((
            (moments_in, moments), (coarse_in, coarse_tables), (fine_in, fine),
            (wavenumbers_in, wavenumbers), (gain_in, gain), (source_in, source_tables),
            (wave_in, wave_tables_ref),
        ))
    ]
    for copy in loads:
        copy.start()

    def y_at(step):
        return modulo(my_y + step + count_gy, count_gy)

    def z_at(step):
        return modulo(my_z + step + count_gz, count_gz)

    first_rows = ((0, 16), (1, 11), (2, 6))

    def rest_rows(step):
        start, count = first_rows[step]
        spans = [(start + count, rows - start - count)]
        return spans + [(0, start)] if start else spans

    early_kinds, all_kinds = 20, 26
    if count_gz == 2:
        whole = [(22, 2, 1, 1), (24, 2, -1, 1), (0, 8, 1, 0), (8, 8, -1, 0), (16, 6, 0, 1)]
        early = [(22, 2, 1, 1), (24, 2, -1, 1), (0, 6, 1, 0), (8, 6, -1, 0), (16, 4, 0, 1)]
        late = [(6, 2, 1, 0), (14, 2, -1, 0), (20, 2, 0, 1)]
    else:
        early = [
            (22, 1, 1, 1), (23, 1, 1, -1), (24, 1, -1, 1), (25, 1, -1, -1),
            (0, 6, 1, 0), (8, 6, -1, 0), (16, 2, 0, 1), (18, 2, 0, -1),
        ]
        late = [(6, 2, 1, 0), (14, 2, -1, 0), (20, 1, 0, 1), (21, 1, 0, -1)]
        whole = early + late

    def send_rows(step, values, base, messages, spans, sems):
        for kind, kinds, dy, dz in messages:
            for start, count in spans:
                for k in range(kind, kind + kinds) if values else ():
                    send_halo[step, k, start : start + count] = values[k][
                        start - base : start - base + count
                    ]
                part = (step, pl.ds(kind, kinds), pl.ds(start, count))
                pltpu.make_async_remote_copy(
                    src_ref=send_halo.at[part], dst_ref=recv_halo.at[part],
                    send_sem=sems.at[0, step], recv_sem=sems.at[1, step],
                    device_id=(y_at(dy), z_at(dz)), device_id_type=MESH,
                ).start()

    def send_first(step, values, base):
        send_rows(step, values, base, whole, [first_rows[step]], first_sems)

    def send_rest(step, values):
        if step == STEPS - 1:
            send_rows(step, values, 0, whole, rest_rows(step), rest_sems)
            return
        send_rows(step, values, 0, early, rest_rows(step), rest_sems)
        send_rows(step, values, 0, late, rest_rows(step), last_sems)

    def wait_rows(step, ref, kinds, count, sem):
        part = ref.at[step, pl.ds(0, kinds), pl.ds(0, count)]
        pltpu.make_async_copy(part, part, sem).wait()

    def wait_first(step, ref, side):
        wait_rows(step, ref, all_kinds, first_rows[step][1], first_sems.at[side, step])

    def wait_rest(step, ref, side):
        kinds = all_kinds if step == STEPS - 1 else early_kinds
        wait_rows(step, ref, kinds, rows - first_rows[step][1], rest_sems.at[side, step])

    def wait_last(step, ref, side):
        if step == STEPS - 1:
            return
        count = rows - first_rows[step][1]
        wait_rows(step, ref, all_kinds - early_kinds, count, last_sems.at[side, step])

    def send_gather(step):
        def send(i, carry):
            pltpu.make_async_remote_copy(
                src_ref=gathered.at[step, me], dst_ref=gathered.at[step, me],
                send_sem=gather_send.at[step], recv_sem=gather_recv.at[step],
                device_id=peer(devices - i), device_id_type=MESH,
            ).start()
            return carry

        if devices <= 32:
            for i in range(1, devices):
                send(i, 0)
        else:
            lax.fori_loop(1, devices, send, 0)

    def wait_for(ref, sem):
        pltpu.make_async_copy(ref, ref, sem).wait()

    waves_y, waves_z = min(KMAX, count_gy), min(KMAX, count_gz * depth)
    modes = wavenumbers.shape[1]

    def wave_onehot():
        q = modulo(wavenumbers[1:2, :], count_gy) * waves_z
        q = q + modulo(wavenumbers[2:3, :], count_gz * depth)
        index = lax.broadcasted_iota(jnp.int32, (waves_y * waves_z, modes), 0)
        return jnp.where(index == q, 1.0, 0.0)

    def x_onehot():
        index = lax.broadcasted_iota(jnp.int32, (KMAX, modes), 0)
        return jnp.where(index == wavenumbers[0:1, :], 1.0, 0.0)

    def build_filters():
        count_q = waves_y * waves_z
        onehot_q = wave_onehot()
        weighted = split(onehot_q * gain[...])
        onehot_x = x_onehot().astype(BF16)
        onehot_x = jnp.concatenate([onehot_x] * 4, 0)
        energy = dot(weighted[0], onehot_x, 1, 1) + dot(weighted[1], onehot_x, 1, 1)
        energy = energy * gain_scale
        index = lax.broadcasted_iota(jnp.int32, (count_q, LANES), 0)
        wave_y, wave_z = divide(index, waves_z), modulo(index, waves_z)
        length_z = count_gz * depth
        phase_y = modulo(wave_y * my_y, count_gy).astype(F32) * (1.0 / count_gy)
        for t in range(depth):
            phase = modulo(wave_z * (my_z * depth + t), length_z).astype(F32)
            angle = (2.0 * math.pi) * (phase_y + phase * (1.0 / length_z))
            ec, es = energy * jnp.cos(angle), energy * jnp.sin(angle)
            for part, stack in enumerate(((ec, es), (es, -ec))):
                pieces = split(jnp.concatenate(stack, 0))
                table = dot3((source_tables[0], source_tables[1]), pieces, 1, 0)
                filters[2 * t + part] = jnp.where(
                    lane1 < LANES // 2, table[:devices], table[devices:]
                )

    def store_coeffs(spectra):
        half = LANES // 2
        sign = jnp.where((lane1 & KMAX) == 0, -1.0, 1.0)
        blocks = []
        for a in range(3):
            top = jnp.concatenate([spectra[a], pltpu.roll(spectra[a], half, 1)], 0)
            swapped = jnp.where((lane1 & KMAX) == 0, pltpu.roll(top, LANES - KMAX, 1), pltpu.roll(top, KMAX, 1))
            blocks.append(jnp.concatenate([top, sign * swapped], 0)[:, :half])
        stacked = jnp.concatenate(blocks, 1)
        transform = dot3((wave_tables_ref[0], wave_tables_ref[1]), split(stacked), 1, 0) * normalizer
        pieces = split(transform)
        onehot_q = wave_onehot().astype(BF16)
        chosen = dot(pieces[0], onehot_q, 0, 0) + dot(pieces[1], onehot_q, 0, 0)
        onehot_x = x_onehot()
        for a in range(3):
            for part in range(2):
                start = (2 * a + part) * KMAX
                picked = jnp.sum(chosen[start : start + KMAX] * onehot_x, axis=0, keepdims=True)
                coeffs[a, part : part + 1, :] = picked

    def partial_waves(speed, start, count):
        stacked = jnp.concatenate([speed[z][a] for z in range(depth) for a in range(3)], 0)
        coarse = dot_paired(stacked, fine[0])
        table = coarse_tables[0, start : start + count]
        return [
            jnp.sum(coarse[r * count : (r + 1) * count] * table, axis=0, keepdims=True)
            for r in range(3 * depth)
        ]

    def project(step, parts):
        folded = [part + pltpu.roll(part, LANES // 2, 1) for part in parts]
        for a in range(3):
            packed = jnp.where(lane1 < LANES // 2, folded[a], folded[3 + a])
            gathered[step, me, :, a * LANES : (a + 1) * LANES] = packed

    def make_force(spectra):
        inverse_coarse = coarse_tables[1]
        swap_sign = jnp.where((lane1 & KMAX) == 0, 1.0, -1.0)
        outer_sign = jnp.where(lane1 < 3 * KMAX, 1.0, -1.0)
        expanded = []
        for z in range(depth):
            for a in range(3):
                first = jnp.sum(spectra[a] * filters[2 * z], axis=0, keepdims=True)
                second = jnp.sum(spectra[a] * filters[2 * z + 1], axis=0, keepdims=True)
                first = first + pltpu.roll(first, LANES // 2, 1)
                second = second + pltpu.roll(second, LANES // 2, 1)
                both = first + swap_sign * pltpu.roll(second, KMAX, 1)
                row = jnp.where(
                    lane1 < LANES // 2, both, outer_sign * pltpu.roll(both, KMAX, 1)
                )
                expanded.append(inverse_coarse * row)
        force = dot_paired(jnp.concatenate(expanded, 0), fine[1])
        return [
            [force[(3 * z + a) * rows : (3 * z + a + 1) * rows] for a in range(3)]
            for z in range(depth)
        ]

    inside = (-1, 1)

    def halo_values(pops):
        values = {}
        for z in range(2):
            e_in, other = inside[z], pops[1 - z]
            for i, sy in enumerate((1, -1)):
                plus, minus = pops[z][1, sy, 0], pops[z][-1, sy, 0]
                both, crossing = plus + minus, other[0, sy, e_in]
                kind = 8 * i + 3 * z
                values[kind] = (pops[z][0, sy, 0] + both) + crossing
                values[kind + 1] = plus - minus
                values[kind + 2] = crossing
                values[8 * i + 6 + z] = both
                values[22 + 2 * i + z] = other[0, sy, -e_in]
            plus, minus = other[1, 0, -e_in], other[-1, 0, -e_in]
            both = plus + minus
            values[16 + 2 * z] = other[0, 0, -e_in] + both
            values[17 + 2 * z] = plus - minus
            values[20 + z] = both
        return values

    def stream(step, local, start, count):
        span = slice(start, start + count)
        totals = []
        for z in range(depth):
            y = [[recv_halo[step, 8 * i + 3 * z + n, span] for n in range(3)] for i in range(2)]
            totals.append(
                totals_of(
                    [value[span] for value in local[z]], y,
                    [recv_halo[step, 16 + 2 * z + n, span] for n in range(2)],
                    [recv_halo[step, 22 + 2 * i + z, span] for i in range(2)], float(inside[z]),
                )
            )
        return totals, [1.0 / totals[z][0] for z in range(depth)]

    def finish(step, local, start, count, totals, force, inverse):
        span = slice(start, start + count)
        out = []
        for z in range(depth):
            up, down, side = [recv_halo[step, k + z, span] for k in (6, 14, 20)]
            totals[z][4] = local[z][3][span] + (up + down) + side
            piece = [value[span] for value in force[z]]
            out.append(collide(totals[z], piece, inverse[z]))
        return out

    def own_totals(pops):
        out = []
        for z in range(2):
            same = {sx: pops[z][sx, 0, 0] for sx in (0, 1, -1)}
            inner = {sx: pops[1 - z][sx, 0, inside[z]] for sx in (0, 1, -1)}
            out.append(local_totals(same, inner, float(inside[z])))
        return out

    def speeds(layers, inverse):
        return [[layers[z][1 + a] * inverse[z] for a in range(3)] for z in range(depth)]

    for copy in loads[:3]:
        copy.wait()
    layers = [[moments[i, z] for i in range(10)] for z in range(depth)]
    speed = speeds(layers, [1.0 / layers[z][0] for z in range(depth)])
    project(0, partial_waves(speed, 0, rows))
    pops = [populations(layers[z], lane) for z in range(depth)]
    for k, value in halo_values(pops).items():
        send_halo[0, k] = value
    pl.semaphore_wait(barrier, devices - 1)
    send_gather(0)
    send_first(0, None, 0)
    send_rest(0, None)
    for copy in loads[3:]:
        copy.wait()
    build_filters()

    def wait_sent(step):
        wait_for(gathered.at[step, pl.ds(0, devices - 1)], gather_send.at[step])
        wait_first(step, send_halo, 0)
        wait_rest(step, send_halo, 0)
        wait_last(step, send_halo, 0)

    for step in range(STEPS):
        last = step == STEPS - 1
        local = own_totals(pops)
        wait_for(gathered.at[step, pl.ds(0, devices - 1)], gather_recv.at[step])
        spectra = [gathered[step, :, 0, a * LANES : (a + 1) * LANES] for a in range(3)]
        force = make_force(spectra)
        if last:
            store_coeffs(spectra)
            for done in range(STEPS):
                wait_sent(done)
        wait_first(step, recv_halo, 1)
        if not last:
            start, count = (0, 16) if step == 0 else (1, 8)
            totals, inverse = stream(step, local, start, count)
            ahead = finish(step, local, start, count, totals, force, inverse)
            if step == 0:
                ahead_parts = partial_waves(speeds(ahead, inverse), start, count)
            ahead = [populations(ahead[z], lane[:count]) for z in range(depth)]
            send_first(step + 1, halo_values(ahead), start)
        wait_rest(step, recv_halo, 1)
        totals, inverse = stream(step, local, 0, rows)
        if not last:
            moved = [
                [None] + [totals[z][1 + a] + force[z][a] for a in range(3)] for z in range(depth)
            ]
            speed = speeds(moved, inverse)
            if step == 0:
                speed = [[value[count:] for value in speed[z]] for z in range(depth)]
                parts = partial_waves(speed, count, rows - count)
                parts = [one + two for one, two in zip(ahead_parts, parts)]
            else:
                parts = partial_waves(speed, 0, rows)
            project(step + 1, parts)
            send_gather(step + 1)
        wait_last(step, recv_halo, 1)
        results = finish(step, local, 0, rows, totals, force, inverse)
        if last:
            for z in range(depth):
                for i in range(10):
                    final[i, z] = results[z][i]
        else:
            pops = [populations(results[z], lane) for z in range(depth)]
            send_rest(step + 1, halo_values(pops))


def hand_over(final_in, coeffs_in, final_out, coeffs_out, sems):
    copies = [
        pltpu.make_async_copy(final_in, final_out, sems.at[0]),
        pltpu.make_async_copy(coeffs_in, coeffs_out, sems.at[1]),
    ]
    for copy in copies:
        copy.start()
    for copy in copies:
        copy.wait()


def per_device(count_gy, count_gz, moments, wavenumbers, mode_gain):
    depth, height, cells_x = moments.shape[1:]
    assert height == 1 and depth == 2 and cells_x % 1024 == 0 and cells_x >= 4096
    rows = cells_x // LANES
    modes = mode_gain.shape[0]
    devices = count_gy * count_gz
    normalizer = 1.0 / math.sqrt(cells_x * height * depth * devices)
    force_scale = FORCE_GAIN / math.sqrt(2 * modes * devices)
    tables = wave_tables(cells_x) + plane_tables(count_gy, count_gz, depth)
    operands = (moments.reshape(10, depth, rows, LANES), wavenumbers, mode_gain.reshape(1, modes)) + tables
    vmem = pl.BlockSpec(memory_space=pltpu.VMEM)
    final, coeffs = pl.pallas_call(
        functools.partial(kernel, count_gy, count_gz, force_scale * normalizer, normalizer),
        out_shape=(
            pltpu.VMEM((10, depth, rows, LANES), F32),
            pltpu.VMEM((3, 2, modes), F32),
        ),
        in_specs=[pl.BlockSpec(memory_space=pl.ANY)] * len(operands),
        out_specs=(vmem, vmem),
        scratch_shapes=[pltpu.VMEM(x.shape, x.dtype) for x in operands] + [
            pltpu.SemaphoreType.DMA((len(operands),)),
            pltpu.VMEM((STEPS, devices, 1, 3 * LANES), F32),
            pltpu.VMEM((2 * depth, devices, LANES), F32),
            pltpu.VMEM((STEPS, 26, rows, LANES), F32),
            pltpu.VMEM((STEPS, 26, rows, LANES), F32),
            pltpu.SemaphoreType.DMA((STEPS,)),
            pltpu.SemaphoreType.DMA((STEPS,)),
            pltpu.SemaphoreType.DMA((2, STEPS)),
            pltpu.SemaphoreType.DMA((2, STEPS)),
            pltpu.SemaphoreType.DMA((2, STEPS)),
        ],
        compiler_params=pltpu.CompilerParams(
            collective_id=0, has_side_effects=True, vmem_limit_bytes=60 * 1024 * 1024
        ),
    )(*operands)
    final, coeffs = pl.pallas_call(
        hand_over,
        out_shape=(
            jax.ShapeDtypeStruct(final.shape, F32),
            jax.ShapeDtypeStruct(coeffs.shape, F32),
        ),
        in_specs=[vmem] * 2,
        out_specs=(pl.BlockSpec(memory_space=pl.ANY), pl.BlockSpec(memory_space=pl.ANY)),
        scratch_shapes=[pltpu.SemaphoreType.DMA((2,))],
        compiler_params=pltpu.CompilerParams(vmem_limit_bytes=4 * 1024 * 1024),
    )(final, coeffs)
    return final.reshape(moments.shape), jnp.transpose(coeffs, (1, 0, 2))


def solution(mesh):
    in_specs = (P(None, "gz", "gy", None), P(), P())
    out_specs = (P(None, "gz", "gy", None), P())
    body = functools.partial(per_device, mesh.shape["gy"], mesh.shape["gz"])
    return jax.shard_map(
        body, mesh=mesh, in_specs=in_specs, out_specs=out_specs, check_vma=False
    )
```
